256 devices in a mesh: visit: 8 (over x, core), patch: 32 (over y, z).
Axes of the slice: x: 4, y: 4, z: 8, core: 2. Of those that a mesh axis runs over, the one named last changes fastest.
Arguments:
- exposure: float32 [8, 512, 32768], P('visit', None, 'patch'), may hold values from -6 to 6
- variance: float32 [8, 512, 32768], P('visit', None, 'patch'), may hold values from 0.5 to 4
- col_start: int32 [8, 32768], P('visit', 'patch'), may hold values from 0 to 1018, as said below
- col_weights: float32 [8, 6, 32768], P('visit', None, 'patch')
- row_start: int32 [8, 16384], P('visit', 'patch'), may hold values from 0 to 506, as said below
- row_weights: float32 [8, 6, 16384], P('visit', None, 'patch')
- offsets: int32 [8, 32], P('visit', 'patch'), may hold values from 0 to 256
- basis_coef: float32 [8, 31], P('visit'), may hold values from -4 to 4
Outputs:
- difference: float32 [8, 512, 32768], P('visit', None, 'patch')
- coadd_image: float32 [512, 32768], P(None, 'patch')
The draws below stay inside these ranges and needn't reach their ends.
Inputs may be any that keep to these rules, and one draw needn't show every extreme that they name: The 6 source columns from col_start lie inside the same CCD. The 6 source rows from row_start lie inside the CCD.
All inputs are finite; a program needn't handle non-finite values.
Results may differ from the reference program's by a relative error of at most 0.02.
Values may be sent and summed in bfloat16 or wider, within the bound.
No kernel may reach another device: no remote copies, remote signals or barrier semaphores. Data moves between devices by JAX's collectives and lax.ppermute only.
A program may use at most 128 MiB of HBM per device.

```python
import math
import jax
import jax.numpy as jnp
import numpy as np
from jax import lax

ROWS = 512
COLS = 1024
RADIUS = 10
RESAMPLE_TAPS = 6
KERNELS = 31
VISITS = 8
PATCHES = 32
STRIP_COLS = 32768
MOST_SHIFT = 256


def start_indices(key, length):
    shifted = jax.random.randint(key, (VISITS, PATCHES), 0, 3)
    local = jnp.arange(PATCHES * length) % length
    first = local[None, :] - 3 + jnp.repeat(shifted, length, axis=1)
    return jnp.clip(first, 0, length - RESAMPLE_TAPS).astype(jnp.int32)


def lanczos_weights(fraction):
    position = jnp.arange(RESAMPLE_TAPS).astype(jnp.float32)[None, :, None] - 2.0 - fraction[:, None, :]
    return (jnp.sinc(position) * jnp.sinc(position / 3.0)).astype(jnp.float32)


def draw_col_start(key, part):
    return start_indices(jax.random.fold_in(key, 11), COLS)


def draw_row_start(key, part):
    return start_indices(jax.random.fold_in(key, 12), ROWS)


def draw_col_weights(key, part):
    fraction = jax.random.uniform(jax.random.fold_in(key, 21), (VISITS, PATCHES * COLS), jnp.float32)
    return lanczos_weights(fraction)


def draw_row_weights(key, part):
    fraction = jax.random.uniform(jax.random.fold_in(key, 22), (VISITS, PATCHES * ROWS), jnp.float32)
    return lanczos_weights(fraction)


def draw_offsets(key, part):
    base = jax.random.randint(jax.random.fold_in(key, 31), (VISITS, PATCHES), 0, MOST_SHIFT + 1)
    chosen = jax.random.randint(jax.random.fold_in(key, 32), (VISITS, 1), 0, PATCHES)
    position = jnp.arange(PATCHES)[None, :]
    base = jnp.where(position == chosen, MOST_SHIFT, base)
    base = jnp.where(position == (chosen + 1) % PATCHES, 0, base)
    return base.astype(jnp.int32)


def block_levels(own_key, extent, pieces, least, largest):
    factor_of = 1.0
    for axis_at, parts in pieces:
        draws = jax.random.uniform(jax.random.fold_in(jax.random.fold_in(own_key, 6), axis_at), (parts,), jnp.float32, least / len(pieces), largest / len(pieces))
        factor_of = factor_of * jnp.repeat(jnp.exp(draws), extent[axis_at] // parts).reshape((-1,) + (1,) * (len(extent) - 1 - axis_at))
    return factor_of


def centred(stream_key, extent, spread, reach, cuts=(), dtype=jnp.bfloat16):
    entries = jax.random.normal(stream_key, extent, jnp.float32) * spread
    if len(cuts) > 0:
        entries = block_levels(stream_key, extent, cuts, -0.22, 0.18) * entries
    return jnp.clip(entries, min=-reach, max=reach).astype(dtype)


def setup_inputs(seed: int = 0) -> dict:
    streams_of = jax.random.split(jax.random.key(seed), 9)
    exposure = centred(streams_of[0], (VISITS, ROWS, STRIP_COLS), 1.0, 6.0, ((0, 8), (2, 32)), jnp.float32)
    variance = jnp.clip(jnp.exp(math.log(4.0) - 2.0794415 * jax.random.uniform(streams_of[1], (VISITS, ROWS, STRIP_COLS), jnp.float32) ** block_levels(streams_of[1], (VISITS, ROWS, STRIP_COLS), ((0, 8), (2, 32)), -0.2, 0.2)), 0.5, 4.0)
    col_start = draw_col_start(jax.random.fold_in(streams_of[8], 71), 0)
    col_weights = draw_col_weights(jax.random.fold_in(streams_of[8], 71), 0)
    row_start = draw_row_start(jax.random.fold_in(streams_of[8], 71), 0)
    row_weights = draw_row_weights(jax.random.fold_in(streams_of[8], 71), 0)
    offsets = draw_offsets(jax.random.fold_in(streams_of[8], 71), 0)
    basis_coef = centred(streams_of[7], (VISITS, KERNELS), 0.4, 4.0, ((0, 8),), jnp.float32)
    return {"exposure": exposure, "variance": variance, "col_start": col_start, "col_weights": col_weights, "row_start": row_start, "row_weights": row_weights, "offsets": offsets, "basis_coef": basis_coef}


SPREADS = (0.7, 1.5, 3.0)
DEGREES = (4, 3, 2)

def basis_tables():
    pick_x = np.zeros((31, 12), np.float32)
    pick_y = np.zeros((31, 12), np.float32)
    kernel = 0
    first_row = 0
    for spread_index in range(3):
        degree = DEGREES[spread_index]
        for power_x in range(degree + 1):
            for power_y in range(degree + 1 - power_x):
                pick_x[kernel, first_row + power_x] = 1.0
                pick_y[kernel, first_row + power_y] = 1.0
                kernel += 1
        first_row += degree + 1
    return (pick_x, pick_y)

def factor_table():
    factor_rows = []
    distance = jnp.arange(2 * RADIUS + 1).astype(jnp.float32) - RADIUS
    for spread_value, degree in zip(SPREADS, DEGREES):
        gaussian = jnp.exp(-distance * distance / (2.0 * spread_value * spread_value)) / (spread_value * math.sqrt(2.0 * math.pi))
        for exponent in range(degree + 1):
            factor_rows.append(gaussian * (distance / spread_value) ** exponent)
    return jnp.stack(factor_rows)

def combined_filters(coef_row):
    pick_x, pick_y = basis_tables()
    factors = factor_table()
    across = jnp.einsum('k,kb,ka,at->bt', coef_row, jnp.asarray(pick_y), jnp.asarray(pick_x), factors, precision=lax.Precision.HIGHEST)
    return (across.astype(jnp.bfloat16), factors.astype(jnp.bfloat16))

def resample(source, col_first, col_taps, row_first, row_taps):
    across = sum((col_taps[member][None, :] * jnp.take(source, col_first + member, axis=1) for member in range(col_taps.shape[0])))
    return sum((row_taps[member][:, None] * jnp.take(across, row_first + member, axis=0) for member in range(row_taps.shape[0])))

def psf_match(patch_values, coef_row):
    col_filter, row_filter = combined_filters(coef_row)
    col_filter = lax.optimization_barrier(col_filter).astype(jnp.float32)
    row_filter = lax.optimization_barrier(row_filter).astype(jnp.float32)
    strip = jnp.concatenate([patch_values[:, -RADIUS:], patch_values, patch_values[:, :RADIUS]], axis=1)[None, None]
    kernel_cols = col_filter[:, ::-1][:, None, None, :]
    along = lax.conv_general_dilated(strip, kernel_cols, (1, 1), 'VALID', dimension_numbers=('NCHW', 'OIHW', 'NCHW'), precision=lax.Precision.HIGHEST)
    along = lax.optimization_barrier(along.astype(jnp.bfloat16)).astype(jnp.float32)
    along = jnp.pad(along, ((0, 0), (0, 0), (RADIUS, RADIUS), (0, 0)))
    kernel_rows = row_filter[:, ::-1][None, :, :, None]
    matched = lax.conv_general_dilated(along, kernel_rows, (1, 1), 'VALID', dimension_numbers=('NCHW', 'OIHW', 'NCHW'), precision=lax.Precision.HIGHEST)
    return matched[0, 0]

def per_ccd(values):
    return values.reshape(ROWS, PATCHES, COLS).transpose(1, 0, 2)

def to_strip(values):
    return values.transpose(1, 0, 2).reshape(ROWS, PATCHES * COLS)

def one_visit(inputs):
    exposure_v, variance_v, col_first, col_taps, row_first, row_taps, shift_cols, coef_row = inputs
    col_first_c = col_first.reshape(PATCHES, COLS)
    col_taps_c = col_taps.reshape(RESAMPLE_TAPS, PATCHES, COLS).transpose(1, 0, 2)
    row_first_c = row_first.reshape(PATCHES, ROWS)
    row_taps_c = row_taps.reshape(RESAMPLE_TAPS, PATCHES, ROWS).transpose(1, 0, 2)
    warped = jax.vmap(resample)(per_ccd(exposure_v), col_first_c, col_taps_c, row_first_c, row_taps_c)
    spread_noise = jax.vmap(resample)(per_ccd(variance_v), col_first_c, col_taps_c * col_taps_c, row_first_c, row_taps_c * row_taps_c)
    inverse = 1.0 / spread_noise
    scaled = warped * inverse
    rotate = jax.vmap(lambda field, amount: jnp.roll(field, amount, axis=1))
    scaled_rot = rotate(scaled, shift_cols)
    inverse_rot = rotate(inverse, shift_cols)
    column = jnp.arange(COLS).astype(jnp.int32)[None, None, :]
    mine = column >= shift_cols[:, None, None]
    total_scaled = jnp.where(mine, scaled_rot, 0.0) + jnp.roll(jnp.where(mine, 0.0, scaled_rot), 1, axis=0)
    total_weight = jnp.where(mine, inverse_rot, 0.0) + jnp.roll(jnp.where(mine, 0.0, inverse_rot), 1, axis=0)
    total_scaled = to_strip(total_scaled)
    total_weight = to_strip(total_weight)
    patch_image = (total_scaled / jnp.maximum(total_weight, 0.1)).astype(jnp.bfloat16)
    patch_image = lax.optimization_barrier(patch_image).astype(jnp.float32)
    matched = psf_match(patch_image, coef_row)
    return (matched, total_weight)

def reference(exposure, variance, col_start, col_weights, row_start, row_weights, offsets, basis_coef):
    matched, total_weight = lax.map(one_visit, (exposure, variance, col_start, col_weights, row_start, row_weights, offsets, basis_coef))
    weighted = lax.optimization_barrier((total_weight * matched).astype(jnp.bfloat16)).astype(jnp.float32)
    numerator = lax.optimization_barrier(jnp.sum(weighted, axis=0))
    denominator = lax.optimization_barrier(jnp.sum(lax.optimization_barrier(total_weight.astype(jnp.bfloat16)).astype(jnp.float32), axis=0))
    coadd_image = numerator / jnp.maximum(denominator, 0.1)
    difference = matched - coadd_image[None]
    return (difference, coadd_image)
```

```python
import functools
import math

import jax
import jax.numpy as jnp
import numpy as np
from jax import lax
from jax.experimental import pallas as pl
from jax.experimental.pallas import tpu as pltpu
from jax.sharding import PartitionSpec as P

RADIUS = 10
TAPS = 6
ROWS = 512
COLS = 1024
EDGE = 256
LANES = 128
FILTERS = 12
WINDOW = 160
PAD = 16
SPREADS = (0.7, 1.5, 3.0)
DEGREES = (4, 3, 2)
F32 = jnp.float32
BF16 = jnp.bfloat16
VMEM_LIMIT = 56 * 1024 * 1024


def factor_table():
    distance = np.arange(2 * RADIUS + 1).astype(np.float32) - RADIUS
    rows = []
    for spread, degree in zip(SPREADS, DEGREES):
        gaussian = np.exp(-distance * distance / np.float32(2.0 * spread * spread)) / np.float32(
            spread * math.sqrt(2.0 * math.pi)
        )
        for exponent in range(degree + 1):
            rows.append(gaussian * (distance / np.float32(spread)) ** exponent)
    return np.stack(rows).astype(np.float32)


def kernel_terms():
    terms = [[] for _ in range(FILTERS)]
    kernel = 0
    first = 0
    for degree in DEGREES:
        for i in range(degree + 1):
            for j in range(degree + 1 - i):
                terms[first + j].append((kernel, first + i))
                kernel += 1
        first += degree + 1
    return terms


def row_band():
    factors = factor_table().astype(BF16)
    gap = np.arange(LANES)[:, None] + PAD - np.arange(WINDOW)[None, :]
    inside = np.abs(gap) <= RADIUS
    at = np.clip(gap + RADIUS, 0, 2 * RADIUS)
    band = np.where(inside[None], factors[:, at], np.zeros((), BF16))
    return band.transpose(1, 0, 2).reshape(LANES, FILTERS * WINDOW).astype(BF16)


def dot(a, b):
    return jnp.dot(a, b, preferred_element_type=F32)


def build_cols(table, low, width, cols_ref, square_ref):
    first = table[0:1, low : low + width]

    @pl.loop(0, COLS // LANES)
    def _(block):
        at = pl.multiple_of(block * LANES, LANES)
        source = lax.broadcasted_iota(jnp.int32, (LANES, width), 0).astype(F32)
        gap = source - (first - (block * LANES).astype(F32))
        value = jnp.zeros((LANES, width), F32)
        for tap in range(TAPS):
            value = jnp.where(gap == float(tap), table[tap + 1 : tap + 2, low : low + width], value)
        cols_ref[pl.ds(at, LANES), :] = value.astype(BF16)
        square_ref[pl.ds(at, LANES), :] = (value * value).astype(BF16)


def build_rows(row_start_ref, row_weights_ref, flip_ref, rows_ref, square_ref):
    flip_ref[...] = jnp.zeros_like(flip_ref)
    flip_ref[0:1, :] = row_start_ref[...].astype(F32)
    flip_ref[1 : TAPS + 1, :] = row_weights_ref[...]
    for block in range(ROWS // LANES):
        at = slice(block * LANES, (block + 1) * LANES)
        turned = jnp.transpose(flip_ref[:, at])
        gap = lax.broadcasted_iota(jnp.int32, (LANES, ROWS), 1).astype(F32) - turned[:, 0:1]
        value = jnp.zeros((LANES, ROWS), F32)
        for tap in range(TAPS):
            value = jnp.where(gap == float(tap), turned[:, tap + 1 : tap + 2], value)
        rows_ref[at, :] = value.astype(BF16)
        square_ref[at, :] = (value * value).astype(BF16)


def rolled_table(col_start_ref, col_weights_ref, table_ref, shift):
    table_ref[...] = jnp.zeros_like(table_ref)
    table_ref[0:1, :] = col_start_ref[...].astype(F32)
    table_ref[1 : TAPS + 1, :] = col_weights_ref[...]
    return pltpu.roll(table_ref[...], shift, 1)


def edge_kernel(
    offset_ref, pixels_ref, noise_ref, col_start_ref, col_weights_ref, row_start_ref, row_weights_ref,
    send_ref, head_ref, own_ref, sent_ref, last_weight_ref, last_patch_ref, rows_ref, rows2_ref,
    table_ref, flip_ref, cols_ref, cols2_ref,
):
    shift = offset_ref[0, 0]
    table = rolled_table(col_start_ref, col_weights_ref, table_ref, shift)
    build_rows(row_start_ref, row_weights_ref, flip_ref, rows_ref, rows2_ref)
    parts = jnp.concatenate([table[:, :EDGE], table[:, COLS - LANES :]], axis=1)
    build_cols(parts, 0, EDGE + LANES, cols_ref, cols2_ref)
    across = dot(pixels_ref[...].astype(BF16), cols_ref[...]).astype(BF16)
    across2 = dot(noise_ref[...].astype(BF16), cols2_ref[...]).astype(BF16)
    warped = dot(rows_ref[...], across)
    inverse = 1.0 / dot(rows2_ref[...], across2)
    scaled = warped * inverse
    mine = lax.broadcasted_iota(jnp.int32, (ROWS, EDGE), 1) >= shift
    edge_scaled = scaled[:, :EDGE]
    edge_inverse = inverse[:, :EDGE]
    own_scaled = jnp.where(mine, edge_scaled, 0.0)
    own_weight = jnp.where(mine, edge_inverse, 0.0)
    sent_scaled = jnp.where(mine, 0.0, edge_scaled)
    sent_weight = jnp.where(mine, 0.0, edge_inverse)
    own_ref[0:ROWS, :] = own_scaled
    own_ref[ROWS : 2 * ROWS, :] = own_weight
    send_ref[0:ROWS, :] = sent_scaled.astype(BF16)
    send_ref[ROWS : 2 * ROWS, :] = sent_weight.astype(BF16)
    head_ref[0:16, :] = jnp.transpose(own_scaled[:, :LANES])[0:16].astype(BF16)
    head_ref[16:32, :] = jnp.transpose(own_weight[:, :LANES])[0:16].astype(BF16)
    sent_ref[0:16, :] = jnp.transpose(sent_scaled[:, :LANES])[0:16]
    sent_ref[16:32, :] = jnp.transpose(sent_weight[:, :LANES])[0:16]
    last_inverse = inverse[:, EDGE:]
    last = scaled[:, EDGE:] / jnp.maximum(last_inverse, 0.1)
    last_weight_ref[...] = last_inverse.astype(BF16)
    last_patch_ref[...] = last.astype(BF16)
    tail = jnp.transpose(last)[LANES - 16 :].astype(BF16)
    send_ref[2 * ROWS : 2 * ROWS + 16, :] = tail[:, :256]
    send_ref[2 * ROWS + 16 :, :] = tail[:, 256:]


def middle_kernel(
    offset_ref, coef_ref, pixels_ref, noise_ref, col_start_ref, col_weights_ref, rows_ref, rows2_ref,
    last_patch_ref, last_weight_ref, factors_ref,
    patch_ref, weight_ref, taps_ref,
    table_ref, cols_ref, cols2_ref,
):
    shift = offset_ref[0, 0]
    width = COLS - EDGE - LANES
    table = rolled_table(col_start_ref, col_weights_ref, table_ref, shift)
    build_cols(table, EDGE, width, cols_ref, cols2_ref)
    across = dot(pixels_ref[...].astype(BF16), cols_ref[...]).astype(BF16)
    across2 = dot(noise_ref[...].astype(BF16), cols2_ref[...]).astype(BF16)
    warped = dot(rows_ref[...], across)
    inverse = 1.0 / dot(rows2_ref[...], across2)
    patch = (warped * inverse) / jnp.maximum(inverse, 0.1)
    weight_ref[:, :width] = inverse.astype(BF16)
    weight_ref[:, width:] = last_weight_ref[...]
    wide = jnp.concatenate([patch, last_patch_ref[...].astype(F32), jnp.zeros((ROWS, LANES), F32)], axis=1)
    patch_ref[...] = pltpu.roll(wide, RADIUS, 1).astype(BF16)
    below = lax.broadcasted_iota(jnp.int32, (LANES, LANES), 1) <= lax.broadcasted_iota(jnp.int32, (LANES, LANES), 0)
    for b, terms in enumerate(kernel_terms()):
        line = sum(coef_ref[0, k] * factors_ref[a : a + 1, :] for k, a in terms)
        line = line.astype(BF16).astype(F32)
        spread = pltpu.roll(jnp.broadcast_to(line, (LANES, LANES)), 0, 1, stride=1, stride_axis=0)
        lanes = slice(b * LANES, (b + 1) * LANES)
        taps_ref[:LANES, lanes] = jnp.where(below, spread, 0.0).astype(BF16)
        taps_ref[LANES:, lanes] = jnp.where(below, 0.0, spread).astype(BF16)


def convolve(window, taps_ref, band_ref, along_ref):
    for half in range(2):
        source = window(half)
        for piece in range(FILTERS // 2):
            lanes = slice(piece * 2 * LANES, (piece + 1) * 2 * LANES)
            along = dot(source, taps_ref[:, lanes]).astype(BF16)
            at = slice(half * LANES, (half + 1) * LANES)
            along_ref[2 * piece, PAD : PAD + ROWS, at] = along[:, :LANES]
            along_ref[2 * piece + 1, PAD : PAD + ROWS, at] = along[:, LANES:]
    for block in range(ROWS // LANES):
        source = jnp.concatenate(
            [along_ref[a, block * LANES : block * LANES + WINDOW, :] for a in range(FILTERS)], axis=0
        )
        yield block, dot(band_ref[...], source)


def clear_margins(along_ref):
    for a in range(FILTERS):
        along_ref[a, 0:PAD, :] = jnp.zeros((PAD, 2 * LANES), BF16)
        along_ref[a, PAD + ROWS :, :] = jnp.zeros((PAD, 2 * LANES), BF16)


def inner_kernel(patch_ref, weight_ref, taps_ref, band_ref, matched_ref, term_ref, along_ref):
    clear_margins(along_ref)

    @pl.loop(0, 2)
    def _(pair):
        start = pl.multiple_of(pair * 2 * LANES, 2 * LANES)

        def window(half):
            at = pl.multiple_of(start + LANES + half * LANES, LANES)
            return patch_ref[:, pl.ds(at, 2 * LANES)]

        for block, matched in convolve(window, taps_ref, band_ref, along_ref):
            rows = slice(block * LANES, (block + 1) * LANES)
            matched_ref[rows, pl.ds(start, 2 * LANES)] = matched
            weight = weight_ref[rows, pl.ds(pl.multiple_of(start + LANES, LANES), 2 * LANES)].astype(F32)
            term_ref[rows, pl.ds(start, 2 * LANES)] = (weight * matched).astype(BF16)


def outer_kernel(
    got_ref, ahead_ref, own_ref, sent_ref, patch_ref, weight_ref, taps_ref, band_ref, term_ref,
    matched_ref, terms_ref,
    along_ref, padded_ref, flip_ref, first_ref,
):
    clear_margins(along_ref)
    total_scaled = own_ref[0:ROWS, :] + got_ref[0:ROWS, :].astype(F32)
    total_weight = own_ref[ROWS : 2 * ROWS, :] + got_ref[ROWS : 2 * ROWS, :].astype(F32)
    patch = total_scaled / jnp.maximum(total_weight, 0.1)
    first_ref[...] = total_weight.astype(BF16)
    lane = lax.broadcasted_iota(jnp.int32, (ROWS, LANES), 1)
    flip_ref[...] = jnp.zeros_like(flip_ref)
    flip_ref[LANES - 16 :, :256] = got_ref[2 * ROWS : 2 * ROWS + 16, :].astype(F32)
    flip_ref[LANES - 16 :, 256:] = got_ref[2 * ROWS + 16 :, :].astype(F32)
    left = jnp.transpose(flip_ref[...])
    wide = pltpu.roll(jnp.concatenate([patch, left], axis=1), RADIUS, 1)
    padded_ref[:, :EDGE] = wide[:, :EDGE].astype(BF16)
    padded_ref[:, EDGE : EDGE + LANES] = jnp.where(
        lane < RADIUS, wide[:, EDGE:], patch_ref[:, :LANES].astype(F32)
    ).astype(BF16)
    padded_ref[:, EDGE + LANES : COLS] = patch_ref[:, LANES : COLS - EDGE]
    near_scaled = ahead_ref[0:16, :].astype(F32) + sent_ref[0:16, :]
    near_weight = ahead_ref[16:32, :].astype(F32) + sent_ref[16:32, :]
    flip_ref[0:16, :] = near_scaled / jnp.maximum(near_weight, 0.1)
    right = pltpu.roll(jnp.transpose(flip_ref[...]), RADIUS, 1)
    padded_ref[:, COLS:] = jnp.where(
        (lane >= RADIUS) & (lane < 2 * RADIUS), right,
        jnp.where(lane < RADIUS, patch_ref[:, COLS - EDGE :].astype(F32), 0.0),
    ).astype(BF16)

    for k in range(8):
        rows = slice(64 * k, 64 * k + 64)
        terms_ref[128 * k + 64 : 128 * k + 128, :EDGE] = first_ref[rows, :]
        terms_ref[128 * k + 64 : 128 * k + 128, EDGE:] = weight_ref[rows, :]
        terms_ref[128 * k : 128 * k + 64, 3 * LANES : 7 * LANES] = term_ref[rows, :]

    @pl.loop(0, 2)
    def _(pair):
        def place(half):
            return pl.multiple_of(jnp.where(pair == 0, half, 2 + 5 * half) * LANES, LANES)

        for block, matched in convolve(
            lambda half: padded_ref[:, pl.ds(place(half), 2 * LANES)], taps_ref, band_ref, along_ref
        ):
            rows = slice(block * LANES, (block + 1) * LANES)
            matched_ref[rows, pl.ds(pl.multiple_of(pair * 2 * LANES, LANES), 2 * LANES)] = matched
            for half in range(2):
                at = pl.ds(place(half), LANES)
                part = matched[:, half * LANES : (half + 1) * LANES]
                for k in (2 * block, 2 * block + 1):
                    low = 64 * (k - 2 * block)
                    weight = terms_ref[128 * k + 64 : 128 * k + 128, at].astype(F32)
                    terms_ref[128 * k : 128 * k + 64, at] = (weight * part[low : low + 64]).astype(BF16)


def final_kernel(inner_ref, outer_ref, coadd_ref, difference_ref, image_ref):
    image = coadd_ref[...].astype(F32)
    image_ref[...] = image
    difference_ref[:, : 3 * LANES] = outer_ref[:, : 3 * LANES] - image[:, : 3 * LANES]
    difference_ref[:, 3 * LANES : 7 * LANES] = inner_ref[...] - image[:, 3 * LANES : 7 * LANES]
    difference_ref[:, 7 * LANES :] = outer_ref[:, 3 * LANES :] - image[:, 7 * LANES :]


def call(body, outs, scratch, specs, flops, moved, name):
    return pl.pallas_call(
        body,
        out_shape=[jax.ShapeDtypeStruct(shape, dtype) for shape, dtype in outs],
        in_specs=specs,
        out_specs=[pl.BlockSpec(memory_space=pltpu.VMEM) for _ in outs],
        scratch_shapes=scratch,
        compiler_params=pltpu.CompilerParams(vmem_limit_bytes=VMEM_LIMIT),
        cost_estimate=pl.CostEstimate(flops=flops, bytes_accessed=moved, transcendentals=0),
        name=name,
    )


SMEM_SPEC = pl.BlockSpec(memory_space=pltpu.SMEM)
VMEM_SPEC = pl.BlockSpec(memory_space=pltpu.VMEM)


def shifted(x, axis, by):
    size = lax.axis_size(axis)
    return lax.ppermute(x, axis, [(i, (i + by) % size) for i in range(size)])


def per_device(
    exposure, variance, col_start, col_weights, row_start, row_weights, offsets, basis_coef
):
    pixels = exposure[0]
    noise = variance[0]
    col_taps = col_weights[0]
    row_taps = row_weights[0]
    factors = np.zeros((16, LANES), np.float32)
    factors[:FILTERS, : 2 * RADIUS + 1] = factor_table()
    factors = np.roll(factors, -2 * RADIUS, axis=1)
    band = jnp.asarray(row_band())
    width = EDGE + LANES
    send, head, own, sent, last_weight, last_patch, rows, rows2 = call(
        edge_kernel,
        [
            ((2 * ROWS + 32, EDGE), BF16),
            ((32, ROWS), BF16),
            ((2 * ROWS, EDGE), F32),
            ((32, ROWS), F32),
            ((ROWS, LANES), BF16),
            ((ROWS, LANES), BF16),
            ((ROWS, ROWS), BF16),
            ((ROWS, ROWS), BF16),
        ],
        [
            pltpu.VMEM((8, COLS), F32),
            pltpu.VMEM((LANES, ROWS), F32),
            pltpu.VMEM((COLS, width), BF16),
            pltpu.VMEM((COLS, width), BF16),
        ],
        [SMEM_SPEC] + [VMEM_SPEC] * 6,
        4 * ROWS * width * (COLS + ROWS),
        8 << 20,
        "edge_columns",
    )(offsets, pixels, noise, col_start, col_taps, row_start, row_taps)
    got = shifted(send, "patch", 1)
    ahead = shifted(head, "patch", -1)
    width = COLS - EDGE - LANES
    patch, weight, taps = call(
        middle_kernel,
        [
            ((ROWS, COLS - EDGE + LANES), BF16),
            ((ROWS, COLS - EDGE), BF16),
            ((2 * LANES, FILTERS * LANES), BF16),
        ],
        [
            pltpu.VMEM((8, COLS), F32),
            pltpu.VMEM((COLS, width), BF16),
            pltpu.VMEM((COLS, width), BF16),
        ],
        [SMEM_SPEC] * 2 + [VMEM_SPEC] * 9,
        4 * ROWS * width * (COLS + ROWS),
        8 << 20,
        "middle_columns",
    )(offsets, basis_coef, pixels, noise, col_start, col_taps, rows, rows2, last_patch, last_weight, jnp.asarray(factors))
    along = pltpu.VMEM((FILTERS, ROWS + 2 * PAD, 2 * LANES), BF16)
    conv_flops = 2 * ROWS * ROWS * FILTERS * (2 * LANES + WINDOW)
    inner, term = call(
        inner_kernel,
        [((ROWS, 4 * LANES), F32), ((ROWS, 4 * LANES), BF16)],
        [along],
        [VMEM_SPEC] * 4,
        conv_flops,
        8 << 20,
        "inner_match",
    )(patch, weight, taps, band)
    outer, terms = call(
        outer_kernel,
        [((ROWS, 4 * LANES), F32), ((2 * ROWS, COLS), BF16)],
        [
            along,
            pltpu.VMEM((ROWS, COLS + LANES), BF16),
            pltpu.VMEM((LANES, ROWS), F32),
            pltpu.VMEM((ROWS, EDGE), BF16),
        ],
        [VMEM_SPEC] * 9,
        conv_flops,
        8 << 20,
        "outer_match",
    )(got, ahead, own, sent, patch, weight, taps, band, term)
    summed = lax.psum_scatter(terms, "visit", scatter_dimension=0, tiled=True).astype(F32)
    piece = summed[:64] / jnp.maximum(summed[64:], 0.1)
    coadd = lax.all_gather(piece.astype(BF16), "visit", axis=0, tiled=True)
    difference, image = call(
        final_kernel,
        [((ROWS, COLS), F32), ((ROWS, COLS), F32)],
        [],
        [VMEM_SPEC] * 3,
        2 * ROWS * COLS,
        8 << 20,
        "difference",
    )(inner, outer, coadd)
    return (difference[None], image)


def solution(mesh):
    return jax.shard_map(
        per_device,
        mesh=mesh,
        in_specs=(
            P("visit", None, "patch"),
            P("visit", None, "patch"),
            P("visit", "patch"),
            P("visit", None, "patch"),
            P("visit", "patch"),
            P("visit", None, "patch"),
            P("visit", "patch"),
            P("visit", None),
        ),
        out_specs=(P("visit", None, "patch"), P(None, "patch")),
        check_vma=False,
    )
```

```python
import functools
import math

import jax
import jax.numpy as jnp
import numpy as np
from jax import lax
from jax.experimental import pallas as pl
from jax.experimental.pallas import tpu as pltpu
from jax.sharding import PartitionSpec as P

RADIUS = 10
TAPS = 6
ROWS = 512
COLS = 1024
EDGE = 256
LANES = 128
FILTERS = 12
WINDOW = 160
PAD = 16
SPREADS = (0.7, 1.5, 3.0)
DEGREES = (4, 3, 2)
F32 = jnp.float32
BF16 = jnp.bfloat16
VMEM_LIMIT = 28 * 1024 * 1024


def factor_table():
    distance = np.arange(2 * RADIUS + 1).astype(np.float32) - RADIUS
    rows = []
    for spread, degree in zip(SPREADS, DEGREES):
        gaussian = np.exp(-distance * distance / np.float32(2.0 * spread * spread)) / np.float32(
            spread * math.sqrt(2.0 * math.pi)
        )
        for exponent in range(degree + 1):
            rows.append(gaussian * (distance / np.float32(spread)) ** exponent)
    return np.stack(rows).astype(np.float32)


def kernel_terms():
    terms = [[] for _ in range(FILTERS)]
    kernel = 0
    first = 0
    for degree in DEGREES:
        for i in range(degree + 1):
            for j in range(degree + 1 - i):
                terms[first + j].append((kernel, first + i))
                kernel += 1
        first += degree + 1
    return terms


def row_band():
    factors = factor_table().astype(BF16)
    gap = np.arange(LANES)[:, None] + PAD - np.arange(WINDOW)[None, :]
    inside = np.abs(gap) <= RADIUS
    at = np.clip(gap + RADIUS, 0, 2 * RADIUS)
    band = np.where(inside[None], factors[:, at], np.zeros((), BF16))
    return band.transpose(1, 0, 2).reshape(LANES, FILTERS * WINDOW).astype(BF16)


def dot(a, b):
    return jnp.dot(a, b, preferred_element_type=F32)


def build_cols(table, low, width, cols_ref, square_ref):
    first = table[0:1, low : low + width]

    @pl.loop(0, COLS // LANES)
    def _(block):
        at = pl.multiple_of(block * LANES, LANES)
        source = lax.broadcasted_iota(jnp.int32, (LANES, width), 0).astype(F32)
        gap = source - (first - (block * LANES).astype(F32))
        value = jnp.zeros((LANES, width), F32)
        for tap in range(TAPS):
            value = jnp.where(gap == float(tap), table[tap + 1 : tap + 2, low : low + width], value)
        cols_ref[pl.ds(at, LANES), :] = value.astype(BF16)
        square_ref[pl.ds(at, LANES), :] = (value * value).astype(BF16)


def build_rows(row_start_ref, row_weights_ref, flip_ref, rows_ref, square_ref):
    flip_ref[...] = jnp.zeros_like(flip_ref)
    flip_ref[0:1, :] = row_start_ref[...].astype(F32)
    for tap in range(TAPS):
        flip_ref[tap + 1 : tap + 2, :] = row_weights_ref[tap]
    for block in range(ROWS // LANES):
        at = slice(block * LANES, (block + 1) * LANES)
        turned = jnp.transpose(flip_ref[:, at])
        gap = lax.broadcasted_iota(jnp.int32, (LANES, ROWS), 1).astype(F32) - turned[:, 0:1]
        value = jnp.zeros((LANES, ROWS), F32)
        for tap in range(TAPS):
            value = jnp.where(gap == float(tap), turned[:, tap + 1 : tap + 2], value)
        rows_ref[at, :] = value.astype(BF16)
        square_ref[at, :] = (value * value).astype(BF16)


def rolled_table(col_start_ref, col_weights_ref, table_ref, shift):
    table_ref[...] = jnp.zeros_like(table_ref)
    table_ref[0:1, :] = col_start_ref[...].astype(F32)
    for tap in range(TAPS):
        table_ref[tap + 1 : tap + 2, :] = col_weights_ref[tap]
    return pltpu.roll(table_ref[...], shift, 1)


def edge_kernel(
    offset_ref, pixels_ref, noise_ref, col_start_ref, col_weights_ref, row_start_ref, row_weights_ref,
    send_ref, head_ref, own_ref, sent_ref, last_weight_ref, last_patch_ref, rows_ref, rows2_ref,
    table_ref, flip_ref, cols_ref, cols2_ref, held_ref, held2_ref, sems,
):
    load = pltpu.make_async_copy(pixels_ref, held_ref, sems.at[0])
    load2 = pltpu.make_async_copy(noise_ref, held2_ref, sems.at[1])
    load.start()
    load2.start()
    shift = offset_ref[0, 0]
    table = rolled_table(col_start_ref, col_weights_ref, table_ref, shift)
    build_rows(row_start_ref, row_weights_ref, flip_ref, rows_ref, rows2_ref)
    parts = jnp.concatenate([table[:, :EDGE], table[:, COLS - LANES :]], axis=1)
    build_cols(parts, 0, EDGE + LANES, cols_ref, cols2_ref)
    load.wait()
    across = dot(held_ref[...].astype(BF16), cols_ref[...]).astype(BF16)
    load2.wait()
    across2 = dot(held2_ref[...].astype(BF16), cols2_ref[...]).astype(BF16)
    warped = dot(rows_ref[...], across)
    inverse = 1.0 / dot(rows2_ref[...], across2)
    scaled = warped * inverse
    mine = lax.broadcasted_iota(jnp.int32, (ROWS, EDGE), 1) >= shift
    edge_scaled = scaled[:, :EDGE]
    edge_inverse = inverse[:, :EDGE]
    own_scaled = jnp.where(mine, edge_scaled, 0.0)
    own_weight = jnp.where(mine, edge_inverse, 0.0)
    sent_scaled = jnp.where(mine, 0.0, edge_scaled)
    sent_weight = jnp.where(mine, 0.0, edge_inverse)
    own_ref[0:ROWS, :] = own_scaled
    own_ref[ROWS : 2 * ROWS, :] = own_weight
    send_ref[0:ROWS, :] = sent_scaled.astype(BF16)
    send_ref[ROWS : 2 * ROWS, :] = sent_weight.astype(BF16)
    head_ref[0:16, :] = jnp.transpose(own_scaled[:, :LANES])[0:16].astype(BF16)
    head_ref[16:32, :] = jnp.transpose(own_weight[:, :LANES])[0:16].astype(BF16)
    sent_ref[0:16, :] = jnp.transpose(sent_scaled[:, :LANES])[0:16]
    sent_ref[16:32, :] = jnp.transpose(sent_weight[:, :LANES])[0:16]
    last_inverse = inverse[:, EDGE:]
    last = scaled[:, EDGE:] / jnp.maximum(last_inverse, 0.1)
    last_weight_ref[...] = last_inverse.astype(BF16)
    last_patch_ref[...] = last.astype(BF16)
    tail = jnp.transpose(last)[LANES - 16 :].astype(BF16)
    send_ref[2 * ROWS : 2 * ROWS + 16, :] = tail[:, :256]
    send_ref[2 * ROWS + 16 :, :] = tail[:, 256:]


def middle_kernel(
    offset_ref, coef_ref, pixels_ref, noise_ref, col_start_ref, col_weights_ref, rows_ref, rows2_ref,
    last_patch_ref, last_weight_ref, factors_ref,
    patch_ref, weight_ref, taps_ref,
    table_ref, cols_ref, cols2_ref,
):
    shift = offset_ref[0, 0]
    width = COLS - EDGE - LANES
    table = rolled_table(col_start_ref, col_weights_ref, table_ref, shift)
    build_cols(table, EDGE, width, cols_ref, cols2_ref)
    across = dot(pixels_ref[...].astype(BF16), cols_ref[...]).astype(BF16)
    across2 = dot(noise_ref[...].astype(BF16), cols2_ref[...]).astype(BF16)
    warped = dot(rows_ref[...], across)
    inverse = 1.0 / dot(rows2_ref[...], across2)
    patch = (warped * inverse) / jnp.maximum(inverse, 0.1)
    weight_ref[:, :width] = inverse.astype(BF16)
    weight_ref[:, width:] = last_weight_ref[...]
    wide = jnp.concatenate([patch, last_patch_ref[...].astype(F32), jnp.zeros((ROWS, LANES), F32)], axis=1)
    patch_ref[...] = pltpu.roll(wide, RADIUS, 1).astype(BF16)
    below = lax.broadcasted_iota(jnp.int32, (LANES, LANES), 1) <= lax.broadcasted_iota(jnp.int32, (LANES, LANES), 0)
    for b, terms in enumerate(kernel_terms()):
        line = sum(coef_ref[0, k] * factors_ref[a : a + 1, :] for k, a in terms)
        line = line.astype(BF16).astype(F32)
        spread = pltpu.roll(jnp.broadcast_to(line, (LANES, LANES)), 0, 1, stride=1, stride_axis=0)
        lanes = slice(b * LANES, (b + 1) * LANES)
        taps_ref[:LANES, lanes] = jnp.where(below, spread, 0.0).astype(BF16)
        taps_ref[LANES:, lanes] = jnp.where(below, 0.0, spread).astype(BF16)


def row_block(step):
    core = lax.axis_index("visit") % 2
    return pl.multiple_of(((step + 2 * core) % 4) * LANES, LANES)


def convolve(window, taps_ref, band_ref, along_ref):
    for half in range(2):
        source = window(half)
        for piece in range(FILTERS // 2):
            lanes = slice(piece * 2 * LANES, (piece + 1) * 2 * LANES)
            along = dot(source, taps_ref[:, lanes]).astype(BF16)
            at = slice(half * LANES, (half + 1) * LANES)
            along_ref[2 * piece, PAD : PAD + ROWS, at] = along[:, :LANES]
            along_ref[2 * piece + 1, PAD : PAD + ROWS, at] = along[:, LANES:]
    for step in range(ROWS // LANES):
        at = row_block(step)
        source = jnp.concatenate([along_ref[a, pl.ds(at, WINDOW), :] for a in range(FILTERS)], axis=0)
        yield step, at, dot(band_ref[...], source)


def clear_margins(along_ref):
    for a in range(FILTERS):
        along_ref[a, 0:PAD, :] = jnp.zeros((PAD, 2 * LANES), BF16)
        along_ref[a, PAD + ROWS :, :] = jnp.zeros((PAD, 2 * LANES), BF16)


def inner_kernel(patch_ref, weight_ref, taps_ref, band_ref, matched_ref, term_ref, along_ref):
    clear_margins(along_ref)

    @pl.loop(0, 2)
    def _(pair):
        start = pl.multiple_of(pair * 2 * LANES, 2 * LANES)

        def window(half):
            at = pl.multiple_of(start + LANES + half * LANES, LANES)
            return patch_ref[:, pl.ds(at, 2 * LANES)]

        for step, at, matched in convolve(window, taps_ref, band_ref, along_ref):
            rows = pl.ds(at, LANES)
            matched_ref[rows, pl.ds(start, 2 * LANES)] = matched
            weight = weight_ref[rows, pl.ds(pl.multiple_of(start + LANES, LANES), 2 * LANES)].astype(F32)
            term_ref[step * LANES : (step + 1) * LANES, pl.ds(start, 2 * LANES)] = (weight * matched).astype(BF16)


def outer_kernel(
    got_ref, ahead_ref, own_ref, sent_ref, patch_ref, weight_ref, taps_ref, band_ref, term_ref,
    matched_ref, keep_ref, give_ref,
    along_ref, padded_ref, flip_ref, first_ref,
):
    clear_margins(along_ref)
    total_scaled = own_ref[0:ROWS, :] + got_ref[0:ROWS, :].astype(F32)
    total_weight = own_ref[ROWS : 2 * ROWS, :] + got_ref[ROWS : 2 * ROWS, :].astype(F32)
    patch = total_scaled / jnp.maximum(total_weight, 0.1)
    first_ref[...] = total_weight.astype(BF16)
    lane = lax.broadcasted_iota(jnp.int32, (ROWS, LANES), 1)
    flip_ref[...] = jnp.zeros_like(flip_ref)
    flip_ref[LANES - 16 :, :256] = got_ref[2 * ROWS : 2 * ROWS + 16, :].astype(F32)
    flip_ref[LANES - 16 :, 256:] = got_ref[2 * ROWS + 16 :, :].astype(F32)
    left = jnp.transpose(flip_ref[...])
    wide = pltpu.roll(jnp.concatenate([patch, left], axis=1), RADIUS, 1)
    padded_ref[:, :EDGE] = wide[:, :EDGE].astype(BF16)
    padded_ref[:, EDGE : EDGE + LANES] = jnp.where(
        lane < RADIUS, wide[:, EDGE:], patch_ref[:, :LANES].astype(F32)
    ).astype(BF16)
    padded_ref[:, EDGE + LANES : COLS] = patch_ref[:, LANES : COLS - EDGE]
    near_scaled = ahead_ref[0:16, :].astype(F32) + sent_ref[0:16, :]
    near_weight = ahead_ref[16:32, :].astype(F32) + sent_ref[16:32, :]
    flip_ref[0:16, :] = near_scaled / jnp.maximum(near_weight, 0.1)
    right = pltpu.roll(jnp.transpose(flip_ref[...]), RADIUS, 1)
    padded_ref[:, COLS:] = jnp.where(
        (lane >= RADIUS) & (lane < 2 * RADIUS), right,
        jnp.where(lane < RADIUS, patch_ref[:, COLS - EDGE :].astype(F32), 0.0),
    ).astype(BF16)

    halves = (keep_ref, keep_ref, give_ref, give_ref)
    for step in range(4):
        for part in range(2):
            low = LANES * (2 * (step % 2) + part)
            rows = pl.ds(pl.multiple_of(row_block(step) + 64 * part, 64), 64)
            halves[step][low + 64 : low + 128, :EDGE] = first_ref[rows, :]
            halves[step][low + 64 : low + 128, EDGE:] = weight_ref[rows, :]
            from_inner = term_ref[step * LANES + 64 * part : step * LANES + 64 * part + 64, :]
            halves[step][low : low + 64, 3 * LANES : 7 * LANES] = from_inner

    @pl.loop(0, 2)
    def _(pair):
        def place(half):
            return pl.multiple_of(jnp.where(pair == 0, half, 2 + 5 * half) * LANES, LANES)

        for step, start, matched in convolve(
            lambda half: padded_ref[:, pl.ds(place(half), 2 * LANES)], taps_ref, band_ref, along_ref
        ):
            matched_ref[pl.ds(start, LANES), pl.ds(pl.multiple_of(pair * 2 * LANES, LANES), 2 * LANES)] = matched
            for half in range(2):
                at = pl.ds(place(half), LANES)
                for part in range(2):
                    low = LANES * (2 * (step % 2) + part)
                    value = matched[64 * part : 64 * part + 64, half * LANES : (half + 1) * LANES]
                    weight = halves[step][low + 64 : low + 128, at].astype(F32)
                    halves[step][low : low + 64, at] = (weight * value).astype(BF16)


def pair_kernel(keep_ref, got_ref, own_ref, one_ref, two_ref, three_ref):
    chip = lax.axis_index("visit") // 2

    def piece(ahead):
        rows = pl.ds(pl.multiple_of(((chip + ahead) % 4) * LANES, LANES), LANES)
        return keep_ref[rows, :].astype(F32) + got_ref[rows, :].astype(F32)

    own_ref[...] = piece(0)
    one_ref[...] = piece(1).astype(BF16)
    two_ref[...] = piece(2).astype(BF16)
    three_ref[...] = piece(3).astype(BF16)


def coadd_kernel(own_ref, one_ref, two_ref, three_ref, coadd_ref):
    total = own_ref[...] + one_ref[...].astype(F32) + two_ref[...].astype(F32) + three_ref[...].astype(F32)
    coadd_ref[...] = (total[:64] / jnp.maximum(total[64:], 0.1)).astype(BF16)


def final_kernel(*refs):
    inner_ref, outer_ref = refs[:2]
    pieces = refs[2:10]
    difference_out, image_out, difference_ref, image_ref, sems = refs[10:]
    index = lax.axis_index("visit")
    chip, core = index // 2, index % 2
    copies = []
    for number, piece_ref in enumerate(pieces):
        side, back = number // 4, number % 4
        start = ((core + side) % 2) * (4 * 64) + ((chip + 4 - back) % 4) * 64
        rows = pl.ds(pl.multiple_of(start, 64), 64)
        image = piece_ref[...].astype(F32)
        image_ref[number] = image
        difference_ref[number, :, : 3 * LANES] = outer_ref[rows, : 3 * LANES] - image[:, : 3 * LANES]
        difference_ref[number, :, 3 * LANES : 7 * LANES] = inner_ref[rows, :] - image[:, 3 * LANES : 7 * LANES]
        difference_ref[number, :, 7 * LANES :] = outer_ref[rows, 3 * LANES :] - image[:, 7 * LANES :]
        for which, (held, out) in enumerate(((image_ref, image_out), (difference_ref, difference_out))):
            copy = pltpu.make_async_copy(held.at[number], out.at[rows, :], sems.at[which, number])
            copy.start()
            copies.append(copy)
    for copy in copies:
        copy.wait()


def call(body, outs, scratch, specs, flops, moved, name, out_spec=None):
    return pl.pallas_call(
        body,
        out_shape=[jax.ShapeDtypeStruct(shape, dtype) for shape, dtype in outs],
        in_specs=specs,
        out_specs=[out_spec or VMEM_SPEC for _ in outs],
        scratch_shapes=scratch,
        compiler_params=pltpu.CompilerParams(vmem_limit_bytes=VMEM_LIMIT),
        cost_estimate=pl.CostEstimate(flops=flops, bytes_accessed=moved, transcendentals=0),
        name=name,
    )


SMEM_SPEC = pl.BlockSpec(memory_space=pltpu.SMEM)
VMEM_SPEC = pl.BlockSpec(memory_space=pltpu.VMEM)
ANY_SPEC = pl.BlockSpec(memory_space=pltpu.HBM)


def shifted(x, axis, by):
    size = lax.axis_size(axis)
    return lax.ppermute(x, axis, [(i, (i + by) % size) for i in range(size)])


def in_hbm(x):
    return pltpu.with_memory_space_constraint(x, pltpu.HBM)


def partner(x):
    return lax.ppermute(x, "visit", [(i, i ^ 1) for i in range(lax.axis_size("visit"))])


def per_device(
    exposure, variance, col_start, col_weights, row_start, row_weights, offsets, basis_coef
):
    pixels = in_hbm(exposure[0])
    noise = in_hbm(variance[0])
    col_taps = in_hbm(jnp.transpose(col_weights, (1, 0, 2)))
    row_taps = in_hbm(jnp.transpose(row_weights, (1, 0, 2)))
    col_start = in_hbm(col_start)
    row_start = in_hbm(row_start)
    factors = np.zeros((16, LANES), np.float32)
    factors[:FILTERS, : 2 * RADIUS + 1] = factor_table()
    factors = np.roll(factors, -2 * RADIUS, axis=1)
    band = jnp.asarray(row_band())
    width = EDGE + LANES
    send, head, own, sent, last_weight, last_patch, rows, rows2 = call(
        edge_kernel,
        [
            ((2 * ROWS + 32, EDGE), BF16),
            ((32, ROWS), BF16),
            ((2 * ROWS, EDGE), F32),
            ((32, ROWS), F32),
            ((ROWS, LANES), BF16),
            ((ROWS, LANES), BF16),
            ((ROWS, ROWS), BF16),
            ((ROWS, ROWS), BF16),
        ],
        [
            pltpu.VMEM((8, COLS), F32),
            pltpu.VMEM((LANES, ROWS), F32),
            pltpu.VMEM((COLS, width), BF16),
            pltpu.VMEM((COLS, width), BF16),
            pltpu.VMEM((ROWS, COLS), F32),
            pltpu.VMEM((ROWS, COLS), F32),
            pltpu.SemaphoreType.DMA((2,)),
        ],
        [SMEM_SPEC] + [ANY_SPEC] * 2 + [VMEM_SPEC] * 4,
        4 * ROWS * width * (COLS + ROWS),
        8 << 20,
        "edge_columns",
    )(offsets, pixels, noise, col_start, col_taps, row_start, row_taps)
    got = shifted(send, "patch", 1)
    ahead = shifted(head, "patch", -1)
    width = COLS - EDGE - LANES
    patch, weight, taps = call(
        middle_kernel,
        [
            ((ROWS, COLS - EDGE + LANES), BF16),
            ((ROWS, COLS - EDGE), BF16),
            ((2 * LANES, FILTERS * LANES), BF16),
        ],
        [
            pltpu.VMEM((8, COLS), F32),
            pltpu.VMEM((COLS, width), BF16),
            pltpu.VMEM((COLS, width), BF16),
        ],
        [SMEM_SPEC] * 2 + [VMEM_SPEC] * 9,
        4 * ROWS * width * (COLS + ROWS),
        8 << 20,
        "middle_columns",
    )(offsets, basis_coef, pixels, noise, col_start, col_taps, rows, rows2, last_patch, last_weight, jnp.asarray(factors))
    along = pltpu.VMEM((FILTERS, ROWS + 2 * PAD, 2 * LANES), BF16)
    conv_flops = 2 * ROWS * ROWS * FILTERS * (2 * LANES + WINDOW)
    inner, term = call(
        inner_kernel,
        [((ROWS, 4 * LANES), F32), ((ROWS, 4 * LANES), BF16)],
        [along],
        [VMEM_SPEC] * 4,
        conv_flops,
        8 << 20,
        "inner_match",
    )(patch, weight, taps, band)
    outer, keep, give = call(
        outer_kernel,
        [((ROWS, 4 * LANES), F32), ((ROWS, COLS), BF16), ((ROWS, COLS), BF16)],
        [
            along,
            pltpu.VMEM((ROWS, COLS + LANES), BF16),
            pltpu.VMEM((LANES, ROWS), F32),
            pltpu.VMEM((ROWS, EDGE), BF16),
        ],
        [VMEM_SPEC] * 9,
        conv_flops,
        8 << 20,
        "outer_match",
    )(got, ahead, own, sent, patch, weight, taps, band, term)
    own_piece, *others = call(
        pair_kernel,
        [((LANES, COLS), F32)] + [((LANES, COLS), BF16)] * 3,
        [],
        [VMEM_SPEC] * 2,
        ROWS * COLS,
        3 << 20,
        "pair_sum",
    )(keep, partner(give))
    others = [shifted(x, "visit", 2 * ahead) for ahead, x in enumerate(others, 1)]
    (piece,) = call(
        coadd_kernel,
        [((64, COLS), BF16)],
        [],
        [VMEM_SPEC] * 4,
        4 * LANES * COLS,
        2 << 20,
        "coadd",
    )(own_piece, *others)
    column = [piece] + [shifted(piece, "visit", 2 * ahead) for ahead in range(1, 4)]
    pieces = column + [partner(x) for x in column]
    difference, image = call(
        final_kernel,
        [((ROWS, COLS), F32), ((ROWS, COLS), F32)],
        [
            pltpu.VMEM((8, 64, COLS), F32),
            pltpu.VMEM((8, 64, COLS), F32),
            pltpu.SemaphoreType.DMA((2, 8)),
        ],
        [VMEM_SPEC] * 10,
        2 * ROWS * COLS,
        8 << 20,
        "difference",
        ANY_SPEC,
    )(inner, outer, *pieces)
    return (difference[None], image)


def solution(mesh):
    return jax.shard_map(
        per_device,
        mesh=mesh,
        in_specs=(
            P("visit", None, "patch"),
            P("visit", None, "patch"),
            P("visit", "patch"),
            P("visit", None, "patch"),
            P("visit", "patch"),
            P("visit", None, "patch"),
            P("visit", "patch"),
            P("visit", None),
        ),
        out_specs=(P("visit", None, "patch"), P(None, "patch")),
        check_vma=False,
    )
```

```python
import functools
import math

import jax
import jax.numpy as jnp
import numpy as np
from jax import lax
from jax.experimental import pallas as pl
from jax.experimental.pallas import tpu as pltpu
from jax.sharding import PartitionSpec as P

RADIUS = 10
TAPS = 6
ROWS = 512
COLS = 1024
EDGE = 256
LANES = 128
FILTERS = 12
WINDOW = 160
PAD = 16
REACH = 272
PIECE = 64
SPREADS = (0.7, 1.5, 3.0)
DEGREES = (4, 3, 2)
F32 = jnp.float32
BF16 = jnp.bfloat16
VMEM_LIMIT = 28 * 1024 * 1024


def factor_table():
    distance = np.arange(2 * RADIUS + 1).astype(np.float32) - RADIUS
    rows = []
    for spread, degree in zip(SPREADS, DEGREES):
        gaussian = np.exp(-distance * distance / np.float32(2.0 * spread * spread)) / np.float32(
            spread * math.sqrt(2.0 * math.pi)
        )
        for exponent in range(degree + 1):
            rows.append(gaussian * (distance / np.float32(spread)) ** exponent)
    return np.stack(rows).astype(np.float32)


def kernel_terms():
    terms = [[] for _ in range(FILTERS)]
    kernel = 0
    first = 0
    for degree in DEGREES:
        for i in range(degree + 1):
            for j in range(degree + 1 - i):
                terms[first + j].append((kernel, first + i))
                kernel += 1
        first += degree + 1
    return terms


def row_band():
    factors = factor_table().astype(BF16)
    gap = np.arange(LANES)[:, None] + PAD - np.arange(WINDOW)[None, :]
    inside = np.abs(gap) <= RADIUS
    at = np.clip(gap + RADIUS, 0, 2 * RADIUS)
    band = np.where(inside[None], factors[:, at], np.zeros((), BF16))
    return band.transpose(1, 0, 2).reshape(LANES, FILTERS * WINDOW).astype(BF16)


def dot(a, b):
    return jnp.dot(a, b, preferred_element_type=F32)


def build_cols(table, low, width, cols_ref, square_ref):
    first = table[0:1, low : low + width]

    @pl.loop(0, COLS // LANES)
    def _(block):
        at = pl.multiple_of(block * LANES, LANES)
        source = lax.broadcasted_iota(jnp.int32, (LANES, width), 0).astype(F32)
        gap = source - (first - (block * LANES).astype(F32))
        value = jnp.zeros((LANES, width), F32)
        for tap in range(TAPS):
            value = jnp.where(gap == float(tap), table[tap + 1 : tap + 2, low : low + width], value)
        cols_ref[pl.ds(at, LANES), :] = value.astype(BF16)
        square_ref[pl.ds(at, LANES), :] = (value * value).astype(BF16)


def build_rows(row_start_ref, row_weights_ref, flip_ref, rows_ref, square_ref):
    flip_ref[...] = jnp.zeros_like(flip_ref)
    flip_ref[0:1, :] = row_start_ref[...].astype(F32)
    for tap in range(TAPS):
        flip_ref[tap + 1 : tap + 2, :] = row_weights_ref[tap]
    for block in range(ROWS // LANES):
        at = slice(block * LANES, (block + 1) * LANES)
        turned = jnp.transpose(flip_ref[:, at])
        gap = lax.broadcasted_iota(jnp.int32, (LANES, ROWS), 1).astype(F32) - turned[:, 0:1]
        value = jnp.zeros((LANES, ROWS), F32)
        for tap in range(TAPS):
            value = jnp.where(gap == float(tap), turned[:, tap + 1 : tap + 2], value)
        rows_ref[at, :] = value.astype(BF16)
        square_ref[at, :] = (value * value).astype(BF16)


def half_start(side):
    core = lax.axis_index("visit") % 2
    half = (core + 1 - side) % 2
    return half, pl.multiple_of(half * (ROWS - REACH), PAD)


def edge_kernel(
    offset_ref, pixels_ref, noise_ref, col_start_ref, col_weights_ref, row_start_ref, row_weights_ref,
    send_ref, rest_ref, edge_ref, last_weight_ref, last_patch_ref, rows_ref, rows2_ref, low_ref, low2_ref, rolled_ref,
    table_ref, flip_ref, cols_ref, cols2_ref, held_ref, held2_ref, whole_ref,
    col_first_ref, col_taps_ref, row_first_ref, row_taps_ref, sems,
):
    loads = [
        pltpu.make_async_copy(source, target, sems.at[number])
        for number, (source, target) in enumerate(
            (
                (row_start_ref, row_first_ref),
                (row_weights_ref, row_taps_ref),
                (col_start_ref, col_first_ref),
                (col_weights_ref, col_taps_ref),
                (pixels_ref, held_ref),
                (noise_ref, held2_ref),
            )
        )
    ]
    for load in loads:
        load.start()
    shift = offset_ref[0, 0]
    for load in loads[:2]:
        load.wait()
    build_rows(row_first_ref, row_taps_ref, flip_ref, rows_ref, rows2_ref)
    for load in loads[2:4]:
        load.wait()
    table_ref[...] = jnp.zeros_like(table_ref)
    table_ref[0:1, :] = col_first_ref[...].astype(F32)
    for tap in range(TAPS):
        table_ref[tap + 1 : tap + 2, :] = col_taps_ref[tap]
    table = pltpu.roll(table_ref[...], shift, 1)
    rolled_ref[...] = table
    parts = jnp.concatenate([table[:, :EDGE], table[:, COLS - LANES :]], axis=1)
    build_cols(parts, 0, EDGE + LANES, cols_ref, cols2_ref)
    loads[4].wait()
    low_ref[...] = held_ref[...].astype(BF16)
    across = dot(low_ref[...], cols_ref[...]).astype(BF16)
    loads[5].wait()
    low2_ref[...] = held2_ref[...].astype(BF16)
    across2 = dot(low2_ref[...], cols2_ref[...]).astype(BF16)
    warped = dot(rows_ref[...], across)
    inverse = 1.0 / dot(rows2_ref[...], across2)
    scaled = warped * inverse
    mine = lax.broadcasted_iota(jnp.int32, (ROWS, EDGE), 1) >= shift
    edge_scaled = scaled[:, :EDGE]
    edge_inverse = inverse[:, :EDGE]
    edge_ref[0:ROWS, :] = edge_scaled
    edge_ref[ROWS:, :] = edge_inverse
    whole_ref[0:ROWS, :] = jnp.where(mine, 0.0, edge_scaled).astype(BF16)
    whole_ref[ROWS:, :] = jnp.where(mine, 0.0, edge_inverse).astype(BF16)
    half, start = half_start(0)
    rest = pl.multiple_of((1 - half) * REACH, PAD)
    send_ref[0:REACH, :] = whole_ref[pl.ds(start, REACH), :]
    send_ref[REACH : 2 * REACH, :] = whole_ref[pl.ds(start + ROWS, REACH), :]
    rest_ref[0 : ROWS - REACH, :] = whole_ref[pl.ds(rest, ROWS - REACH), :]
    rest_ref[ROWS - REACH :, :] = whole_ref[pl.ds(rest + ROWS, ROWS - REACH), :]
    last_inverse = inverse[:, EDGE:]
    last = scaled[:, EDGE:] / jnp.maximum(last_inverse, 0.1)
    last_weight_ref[...] = last_inverse.astype(BF16)
    last_patch_ref[...] = last.astype(BF16)
    tail = jnp.transpose(last)[LANES - 16 :].astype(BF16)
    send_ref[2 * REACH : 2 * REACH + 16, :] = tail[:, :256]
    send_ref[2 * REACH + 16 :, :] = tail[:, 256:]


def middle_kernel(
    offset_ref, coef_ref, low_ref, low2_ref, rolled_ref, rows_ref, rows2_ref,
    last_patch_ref, last_weight_ref, factors_ref, edge_ref,
    patch_ref, weight_ref, taps_ref, head_ref, sent_ref,
    cols_ref, cols2_ref,
):
    turned = jnp.concatenate(
        [jnp.transpose(edge_ref[0:ROWS, :LANES])[0:16], jnp.transpose(edge_ref[ROWS:, :LANES])[0:16]], axis=0
    )
    column = lax.broadcasted_iota(jnp.int32, (32, ROWS), 0) % 16
    head_ref[...] = jnp.where(column >= offset_ref[0, 0], turned, 0.0).astype(BF16)
    sent_ref[...] = jnp.where(column >= offset_ref[0, 0], 0.0, turned)
    width = COLS - EDGE - LANES
    build_cols(rolled_ref[...], EDGE, width, cols_ref, cols2_ref)
    across = dot(low_ref[...], cols_ref[...]).astype(BF16)
    across2 = dot(low2_ref[...], cols2_ref[...]).astype(BF16)
    warped = dot(rows_ref[...], across)
    inverse = 1.0 / dot(rows2_ref[...], across2)
    patch = (warped * inverse) / jnp.maximum(inverse, 0.1)
    weight_ref[:, :width] = inverse.astype(BF16)
    weight_ref[:, width:] = last_weight_ref[...]
    wide = jnp.concatenate([patch, last_patch_ref[...].astype(F32), jnp.zeros((ROWS, LANES), F32)], axis=1)
    patch_ref[...] = pltpu.roll(wide, RADIUS, 1).astype(BF16)
    below = lax.broadcasted_iota(jnp.int32, (LANES, LANES), 1) <= lax.broadcasted_iota(jnp.int32, (LANES, LANES), 0)
    for b, terms in enumerate(kernel_terms()):
        line = sum(coef_ref[0, k] * factors_ref[a : a + 1, :] for k, a in terms)
        line = line.astype(BF16).astype(F32)
        spread = pltpu.roll(jnp.broadcast_to(line, (LANES, LANES)), 0, 1, stride=1, stride_axis=0)
        lanes = slice(b * LANES, (b + 1) * LANES)
        taps_ref[:LANES, lanes] = jnp.where(below, spread, 0.0).astype(BF16)
        taps_ref[LANES:, lanes] = jnp.where(below, 0.0, spread).astype(BF16)


def row_block(step):
    core = lax.axis_index("visit") % 2
    return pl.multiple_of(((step + 2 * core) % 4) * LANES, LANES)


def convolve(window, taps_ref, band_ref, along_ref):
    for half in range(2):
        source = window(half)
        for piece in range(FILTERS // 2):
            lanes = slice(piece * 2 * LANES, (piece + 1) * 2 * LANES)
            along = dot(source, taps_ref[:, lanes]).astype(BF16)
            at = slice(half * LANES, (half + 1) * LANES)
            along_ref[2 * piece, PAD : PAD + ROWS, at] = along[:, :LANES]
            along_ref[2 * piece + 1, PAD : PAD + ROWS, at] = along[:, LANES:]
    for step in range(ROWS // LANES):
        at = row_block(step)
        source = jnp.concatenate([along_ref[a, pl.ds(at, WINDOW), :] for a in range(FILTERS)], axis=0)
        yield step, at, dot(band_ref[...], source)


def clear_margins(along_ref):
    for a in range(FILTERS):
        along_ref[a, 0:PAD, :] = jnp.zeros((PAD, 2 * LANES), BF16)
        along_ref[a, PAD + ROWS :, :] = jnp.zeros((PAD, 2 * LANES), BF16)


def inner_kernel(patch_ref, weight_ref, taps_ref, band_ref, matched_ref, keep_ref, give_ref, along_ref):
    clear_margins(along_ref)
    halves = (keep_ref, keep_ref, give_ref, give_ref)
    for step in range(4):
        low = LANES * (step % 2)
        halves[step][low : low + LANES, 4 * LANES :] = weight_ref[pl.ds(row_block(step), LANES), :]

    @pl.loop(0, 2)
    def _(pair):
        start = pl.multiple_of(pair * 2 * LANES, 2 * LANES)

        def window(half):
            at = pl.multiple_of(start + LANES + half * LANES, LANES)
            return patch_ref[:, pl.ds(at, 2 * LANES)]

        for step, at, matched in convolve(window, taps_ref, band_ref, along_ref):
            rows = pl.ds(at, LANES)
            matched_ref[rows, pl.ds(start, 2 * LANES)] = matched
            weight = weight_ref[rows, pl.ds(pl.multiple_of(start + LANES, LANES), 2 * LANES)].astype(F32)
            low = LANES * (step % 2)
            halves[step][low : low + LANES, pl.ds(start, 2 * LANES)] = (weight * matched).astype(BF16)


def match_half(
    side, offset_ref, scaled, weights, edge_ref, patch_ref, weight_ref, left, right, taps_ref, band_ref,
    matched_ref, term_ref, along_ref, padded_ref, held_ref,
):
    half, start = half_start(side)
    window = pl.ds(start, REACH)
    inside = pl.multiple_of(half * PAD, PAD)
    for a in range(FILTERS):
        along_ref[a, 0:PAD, :] = jnp.zeros((PAD, 2 * LANES), BF16)
        along_ref[a, REACH:, :] = jnp.zeros((PAD, 2 * LANES), BF16)
    mine = lax.broadcasted_iota(jnp.int32, (REACH, EDGE), 1) >= offset_ref[0, 0]
    total_scaled = jnp.where(mine, edge_ref[window, :], 0.0) + scaled.astype(F32)
    total_weight = jnp.where(mine, edge_ref[pl.ds(start + ROWS, REACH), :], 0.0) + weights.astype(F32)
    patch = total_scaled / jnp.maximum(total_weight, 0.1)
    held_ref[:, :EDGE] = total_weight.astype(BF16)
    held_ref[:, EDGE:] = weight_ref[window, :]
    lane = lax.broadcasted_iota(jnp.int32, (REACH, LANES), 1)
    wide = pltpu.roll(jnp.concatenate([patch, left[window, :]], axis=1), RADIUS, 1)
    padded_ref[:, :EDGE] = wide[:, :EDGE].astype(BF16)
    padded_ref[:, EDGE : EDGE + LANES] = jnp.where(
        lane < RADIUS, wide[:, EDGE:], patch_ref[window, :LANES].astype(F32)
    ).astype(BF16)
    padded_ref[:, EDGE + LANES : COLS] = patch_ref[window, LANES : COLS - EDGE]
    padded_ref[:, COLS:] = jnp.where(
        (lane >= RADIUS) & (lane < 2 * RADIUS), right[window, :],
        jnp.where(lane < RADIUS, patch_ref[window, COLS - EDGE :].astype(F32), 0.0),
    ).astype(BF16)
    own = pl.ds(inside, ROWS // 2)
    term_ref[:, 4 * LANES :] = held_ref[own, :EDGE]

    @pl.loop(0, 2)
    def _(pair):
        def place(half):
            return pl.multiple_of(jnp.where(pair == 0, half, 2 + 5 * half) * LANES, LANES)

        for number in range(2):
            source = padded_ref[:, pl.ds(place(number), 2 * LANES)]
            at = slice(number * LANES, (number + 1) * LANES)
            rows = pl.ds(pl.multiple_of(PAD - inside, PAD), REACH)
            for piece in range(FILTERS // 2):
                along = dot(source, taps_ref[:, piece * 2 * LANES : (piece + 1) * 2 * LANES]).astype(BF16)
                along_ref[2 * piece, rows, at] = along[:, :LANES]
                along_ref[2 * piece + 1, rows, at] = along[:, LANES:]
        lanes = pl.ds(pl.multiple_of(pair * 2 * LANES, LANES), 2 * LANES)
        for step in range(2):
            at = slice(step * LANES, (step + 1) * LANES)
            source = jnp.concatenate(
                [along_ref[a, step * LANES : step * LANES + WINDOW, :] for a in range(FILTERS)], axis=0
            )
            matched = dot(band_ref[...], source)
            matched_ref[at, lanes] = matched
            rows = pl.ds(pl.multiple_of(inside + step * LANES, PAD), LANES)
            weight = jnp.concatenate([held_ref[rows, pl.ds(place(number), LANES)] for number in range(2)], axis=1)
            term_ref[at, lanes] = (weight.astype(F32) * matched).astype(BF16)


def given_kernel(
    offset_ref, got_ref, ahead_ref, edge_ref, sent_ref, patch_ref, weight_ref, taps_ref, band_ref,
    matched_ref, term_ref, left_ref, right_ref,
    along_ref, padded_ref, held_ref, flip_ref,
):
    flip_ref[...] = jnp.zeros_like(flip_ref)
    flip_ref[LANES - 16 :, :256] = got_ref[2 * REACH : 2 * REACH + 16, :].astype(F32)
    flip_ref[LANES - 16 :, 256:] = got_ref[2 * REACH + 16 :, :].astype(F32)
    left_ref[...] = jnp.transpose(flip_ref[...])
    near_scaled = ahead_ref[0:16, :].astype(F32) + sent_ref[0:16, :]
    near_weight = ahead_ref[16:32, :].astype(F32) + sent_ref[16:32, :]
    flip_ref[0:16, :] = near_scaled / jnp.maximum(near_weight, 0.1)
    right_ref[...] = pltpu.roll(jnp.transpose(flip_ref[...]), RADIUS, 1)
    match_half(
        0, offset_ref, got_ref[0:REACH, :], got_ref[REACH : 2 * REACH, :], edge_ref, patch_ref, weight_ref,
        left_ref, right_ref, taps_ref, band_ref, matched_ref, term_ref, along_ref, padded_ref, held_ref,
    )


def kept_kernel(
    offset_ref, got_ref, rest_ref, edge_ref, patch_ref, weight_ref, left_ref, right_ref, taps_ref, band_ref,
    matched_ref, term_ref,
    along_ref, padded_ref, held_ref, joined_ref,
):
    half, _ = half_start(1)
    count = ROWS - REACH
    both = REACH - count
    for part in range(2):
        there = pl.multiple_of(part * REACH + half * count, PAD)
        here = pl.multiple_of(part * REACH + (1 - half) * count, PAD)
        joined_ref[pl.ds(here, both), :] = got_ref[pl.ds(there, both), :]
        here = pl.multiple_of(part * REACH + half * both, PAD)
        joined_ref[pl.ds(here, count), :] = rest_ref[part * count : (part + 1) * count, :]
    match_half(
        1, offset_ref, joined_ref[0:REACH, :], joined_ref[REACH:, :], edge_ref, patch_ref, weight_ref,
        left_ref, right_ref, taps_ref, band_ref, matched_ref, term_ref, along_ref, padded_ref, held_ref,
    )


def pair_kernel(keep_ref, got_ref, keep2_ref, got2_ref, own_ref, one_ref, two_ref, three_ref):
    chip = lax.axis_index("visit") // 2
    width = keep_ref.shape[1]
    for ahead, out_ref in enumerate((own_ref, one_ref, two_ref, three_ref)):
        rows = pl.ds(pl.multiple_of(((chip + ahead) % 4) * PIECE, PIECE), PIECE)
        first = keep_ref[rows, :].astype(F32) + got_ref[rows, :].astype(F32)
        second = keep2_ref[rows, :].astype(F32) + got2_ref[rows, :].astype(F32)
        out_ref[:, :width] = first.astype(out_ref.dtype)
        out_ref[:, width:] = second.astype(out_ref.dtype)


def coadd_kernel(own_ref, one_ref, two_ref, three_ref, coadd_ref):
    total = own_ref[...] + one_ref[...].astype(F32) + two_ref[...].astype(F32) + three_ref[...].astype(F32)
    inner, outer = total[:, : COLS + 2 * LANES], total[:, COLS + 2 * LANES :]
    weight = jnp.maximum(jnp.concatenate([outer[:, 4 * LANES :], inner[:, 4 * LANES :]], axis=1), 0.1)
    terms = jnp.concatenate([outer[:, : 3 * LANES], inner[:, : 4 * LANES], outer[:, 3 * LANES : 4 * LANES]], axis=1)
    coadd_ref[...] = (terms / weight).astype(BF16)


def final_kernel(side, *refs):
    inner_ref, outer_ref = refs[:2]
    pieces = refs[2:6]
    difference_out, image_out, difference_ref, image_ref, sems = refs[-5:]
    index = lax.axis_index("visit")
    chip, core = index // 2, index % 2
    copies = []
    for back, piece_ref in enumerate(pieces):
        within = pl.multiple_of(((chip + 4 - back) % 4) * PIECE, PIECE)
        rows = pl.ds(pl.multiple_of(((core + side) % 2) * (4 * PIECE) + within, PIECE), PIECE)
        near = pl.ds(within, PIECE)
        image = piece_ref[...].astype(F32)
        image_ref[back] = image
        difference_ref[back, :, : 3 * LANES] = outer_ref[near, : 3 * LANES] - image[:, : 3 * LANES]
        difference_ref[back, :, 3 * LANES : 7 * LANES] = inner_ref[rows, :] - image[:, 3 * LANES : 7 * LANES]
        difference_ref[back, :, 7 * LANES :] = outer_ref[near, 3 * LANES :] - image[:, 7 * LANES :]
        for which, (held, out) in enumerate(((image_ref, image_out), (difference_ref, difference_out))):
            copy = pltpu.make_async_copy(held.at[back], out.at[rows, :], sems.at[which, back])
            copy.start()
            copies.append(copy)
    for copy in copies:
        copy.wait()


def call(body, outs, scratch, specs, flops, moved, name, out_spec=None, aliases=None):
    return pl.pallas_call(
        body,
        out_shape=[jax.ShapeDtypeStruct(shape, dtype) for shape, dtype in outs],
        in_specs=specs,
        out_specs=[out_spec or VMEM_SPEC for _ in outs],
        scratch_shapes=scratch,
        input_output_aliases=aliases or {},
        compiler_params=pltpu.CompilerParams(vmem_limit_bytes=VMEM_LIMIT),
        cost_estimate=pl.CostEstimate(flops=flops, bytes_accessed=moved, transcendentals=0),
        name=name,
    )


SMEM_SPEC = pl.BlockSpec(memory_space=pltpu.SMEM)
VMEM_SPEC = pl.BlockSpec(memory_space=pltpu.VMEM)
HBM_SPEC = pl.BlockSpec(memory_space=pltpu.HBM)


def shifted(x, axis, by):
    size = lax.axis_size(axis)
    return lax.ppermute(x, axis, [(i, (i + by) % size) for i in range(size)])


def in_hbm(x):
    return pltpu.with_memory_space_constraint(x, pltpu.HBM)


def partner(x):
    return lax.ppermute(x, "visit", [(i, i ^ 1) for i in range(lax.axis_size("visit"))])


def per_device(
    exposure, variance, col_start, col_weights, row_start, row_weights, offsets, basis_coef
):
    pixels = in_hbm(exposure[0])
    noise = in_hbm(variance[0])
    col_taps = in_hbm(jnp.transpose(col_weights, (1, 0, 2)))
    row_taps = in_hbm(jnp.transpose(row_weights, (1, 0, 2)))
    col_start = in_hbm(col_start)
    row_start = in_hbm(row_start)
    factors = np.zeros((16, LANES), np.float32)
    factors[:FILTERS, : 2 * RADIUS + 1] = factor_table()
    factors = np.roll(factors, -2 * RADIUS, axis=1)
    band = jnp.asarray(row_band())
    width = EDGE + LANES
    send, rest, edge, last_weight, last_patch, rows, rows2, low, low2, rolled = call(
        edge_kernel,
        [
            ((2 * REACH + 32, EDGE), BF16),
            ((2 * (ROWS - REACH), EDGE), BF16),
            ((2 * ROWS, EDGE), F32),
            ((ROWS, LANES), BF16),
            ((ROWS, LANES), BF16),
            ((ROWS, ROWS), BF16),
            ((ROWS, ROWS), BF16),
            ((ROWS, COLS), BF16),
            ((ROWS, COLS), BF16),
            ((8, COLS), F32),
        ],
        [
            pltpu.VMEM((8, COLS), F32),
            pltpu.VMEM((LANES, ROWS), F32),
            pltpu.VMEM((COLS, width), BF16),
            pltpu.VMEM((COLS, width), BF16),
            pltpu.VMEM((ROWS, COLS), F32),
            pltpu.VMEM((ROWS, COLS), F32),
            pltpu.VMEM((2 * ROWS, EDGE), BF16),
            pltpu.VMEM((1, COLS), jnp.int32),
            pltpu.VMEM((TAPS, 1, COLS), F32),
            pltpu.VMEM((1, ROWS), jnp.int32),
            pltpu.VMEM((TAPS, 1, ROWS), F32),
            pltpu.SemaphoreType.DMA((6,)),
        ],
        [SMEM_SPEC] + [HBM_SPEC] * 6,
        4 * ROWS * width * (COLS + ROWS),
        8 << 20,
        "edge_columns",
    )(offsets, pixels, noise, col_start, col_taps, row_start, row_taps)
    got = shifted(send, "patch", 1)
    got_rest = shifted(rest, "patch", 1)
    width = COLS - EDGE - LANES
    patch, weight, taps, head, sent = call(
        middle_kernel,
        [
            ((ROWS, COLS - EDGE + LANES), BF16),
            ((ROWS, COLS - EDGE), BF16),
            ((2 * LANES, FILTERS * LANES), BF16),
            ((32, ROWS), BF16),
            ((32, ROWS), F32),
        ],
        [pltpu.VMEM((COLS, width), BF16), pltpu.VMEM((COLS, width), BF16)],
        [SMEM_SPEC] * 2 + [VMEM_SPEC] * 9,
        1 << 20,
        1 << 10,
        "middle_columns",
    )(offsets, basis_coef, low, low2, rolled, rows, rows2, last_patch, last_weight, jnp.asarray(factors), edge)
    ahead = shifted(head, "patch", -1)
    conv_flops = 2 * ROWS * ROWS * FILTERS * (2 * LANES + WINDOW)
    inner_width = COLS + 2 * LANES
    inner, keep, give = call(
        inner_kernel,
        [((ROWS, 4 * LANES), F32), ((ROWS // 2, inner_width), BF16), ((ROWS // 2, inner_width), BF16)],
        [pltpu.VMEM((FILTERS, ROWS + 2 * PAD, 2 * LANES), BF16)],
        [VMEM_SPEC] * 4,
        1 << 20,
        1 << 10,
        "inner_match",
    )(patch, weight, taps, band)
    inner_sum = keep, partner(give)
    outer_width = 4 * LANES + EDGE
    half_outs = [((ROWS // 2, 4 * LANES), F32), ((ROWS // 2, outer_width), BF16)]
    half_scratch = [
        pltpu.VMEM((FILTERS, REACH + PAD, 2 * LANES), BF16),
        pltpu.VMEM((REACH, COLS + LANES), BF16),
        pltpu.VMEM((REACH, COLS), BF16),
    ]
    given, give, left, right = call(
        given_kernel,
        half_outs + [((ROWS, LANES), F32)] * 2,
        half_scratch + [pltpu.VMEM((LANES, ROWS), F32)],
        [SMEM_SPEC] + [VMEM_SPEC] * 8,
        1 << 20,
        1 << 10,
        "given_match",
    )(offsets, got, ahead, edge, sent, patch, weight, taps, band)
    kept, keep = call(
        kept_kernel,
        half_outs,
        half_scratch + [pltpu.VMEM((2 * REACH, EDGE), BF16)],
        [SMEM_SPEC] + [VMEM_SPEC] * 9,
        8 * conv_flops,
        64 << 20,
        "kept_match",
    )(offsets, got, got_rest, edge, patch, weight, left, right, taps, band)
    own_piece, *others = call(
        pair_kernel,
        [((PIECE, inner_width + outer_width), F32)] + [((PIECE, inner_width + outer_width), BF16)] * 3,
        [],
        [VMEM_SPEC] * 4,
        ROWS * COLS,
        3 << 20,
        "pair_sum",
    )(*inner_sum, keep, partner(give))
    others = [shifted(x, "visit", 2 * ahead) for ahead, x in enumerate(others, 1)]
    (piece,) = call(
        coadd_kernel, [((PIECE, COLS), BF16)], [], [VMEM_SPEC] * 4, 8 * PIECE * COLS, 2 << 20, "coadd"
    )(own_piece, *others)
    column = [piece] + [shifted(piece, "visit", 2 * ahead) for ahead in range(1, 4)]
    swapped = [partner(x) for x in column]
    outs = [((ROWS, COLS), F32), ((ROWS, COLS), F32)]
    scratch = [pltpu.VMEM((4, PIECE, COLS), F32), pltpu.VMEM((4, PIECE, COLS), F32), pltpu.SemaphoreType.DMA((2, 4))]
    half_done = call(
        functools.partial(final_kernel, 0), outs, scratch, [VMEM_SPEC] * 6, ROWS * COLS, 4 << 20, "difference_own", HBM_SPEC
    )(inner, kept, *column)
    difference, image = call(
        functools.partial(final_kernel, 1), outs, scratch, [VMEM_SPEC] * 6 + [HBM_SPEC] * 2, ROWS * COLS, 4 << 20,
        "difference_other", HBM_SPEC, {6: 0, 7: 1},
    )(inner, given, *swapped, *half_done)
    return (difference[None], image)


def solution(mesh):
    return jax.shard_map(
        per_device,
        mesh=mesh,
        in_specs=(
            P("visit", None, "patch"),
            P("visit", None, "patch"),
            P("visit", "patch"),
            P("visit", None, "patch"),
            P("visit", "patch"),
            P("visit", None, "patch"),
            P("visit", "patch"),
            P("visit", None),
        ),
        out_specs=(P("visit", None, "patch"), P(None, "patch")),
        check_vma=False,
    )
```

```python
import functools
import math

import jax
import jax.numpy as jnp
import numpy as np
from jax import lax
from jax.experimental import pallas as pl
from jax.experimental.pallas import tpu as pltpu
from jax.sharding import PartitionSpec as P

RADIUS = 10
TAPS = 6
ROWS = 512
COLS = 1024
EDGE = 256
LANES = 128
FILTERS = 12
WINDOW = 160
PAD = 16
REACH = 272
PIECE = 64
SPREADS = (0.7, 1.5, 3.0)
DEGREES = (4, 3, 2)
F32 = jnp.float32
BF16 = jnp.bfloat16
VMEM_LIMIT = 28 * 1024 * 1024


def factor_table():
    distance = np.arange(2 * RADIUS + 1).astype(np.float32) - RADIUS
    rows = []
    for spread, degree in zip(SPREADS, DEGREES):
        gaussian = np.exp(-distance * distance / np.float32(2.0 * spread * spread)) / np.float32(
            spread * math.sqrt(2.0 * math.pi)
        )
        for exponent in range(degree + 1):
            rows.append(gaussian * (distance / np.float32(spread)) ** exponent)
    return np.stack(rows).astype(np.float32)


def kernel_terms():
    terms = [[] for _ in range(FILTERS)]
    kernel = 0
    first = 0
    for degree in DEGREES:
        for i in range(degree + 1):
            for j in range(degree + 1 - i):
                terms[first + j].append((kernel, first + i))
                kernel += 1
        first += degree + 1
    return terms


def row_band():
    factors = factor_table().astype(BF16)
    gap = np.arange(LANES)[:, None] + PAD - np.arange(WINDOW)[None, :]
    inside = np.abs(gap) <= RADIUS
    at = np.clip(gap + RADIUS, 0, 2 * RADIUS)
    band = np.where(inside[None], factors[:, at], np.zeros((), BF16))
    return band.transpose(1, 0, 2).reshape(LANES, FILTERS * WINDOW).astype(BF16)


def dot(a, b):
    return jnp.dot(a, b, preferred_element_type=F32)


def nth_tap(gap):
    return jnp.where((gap & -8) == 0, gap, 7)


def build_cols(table, low, width, cols_ref, square_ref):
    taps = table[:, low : low + width]
    first = taps[TAPS : TAPS + 1].astype(jnp.int32)
    taps = jnp.where(lax.broadcasted_iota(jnp.int32, (8, width), 0) < TAPS, taps, 0.0)
    base = lax.broadcasted_iota(jnp.int32, (8, width), 0) - first

    @pl.loop(0, COLS // LANES)
    def _(block):
        for group in range(LANES // PAD):
            at = block * LANES + group * PAD
            value = jnp.concatenate(
                [jnp.take_along_axis(taps, nth_tap(base + (at + step)), axis=0) for step in (0, 8)], axis=0
            )
            rows = pl.ds(pl.multiple_of(at, PAD), PAD)
            cols_ref[rows, :] = value.astype(BF16)
            square_ref[rows, :] = (value * value).astype(BF16)


def build_rows(row_start_ref, row_weights_ref, flip_ref, rows_ref, square_ref):
    flip_ref[...] = jnp.zeros_like(flip_ref)
    for tap in range(TAPS):
        flip_ref[tap : tap + 1, :] = row_weights_ref[tap]
    flip_ref[8:9, :] = row_start_ref[...].astype(F32)
    for block in range(ROWS // LANES):
        at = slice(block * LANES, (block + 1) * LANES)
        turned = jnp.transpose(flip_ref[:, at])
        lane = lax.broadcasted_iota(jnp.int32, (LANES, LANES), 1)
        base = lane - turned[:, 8:9].astype(jnp.int32)
        for part in range(ROWS // LANES):
            value = jnp.take_along_axis(turned, nth_tap(base + part * LANES), axis=1)
            lanes = slice(part * LANES, (part + 1) * LANES)
            rows_ref[at, lanes] = value.astype(BF16)
            square_ref[at, lanes] = (value * value).astype(BF16)


def half_start(side):
    core = lax.axis_index("visit") % 2
    half = (core + 1 - side) % 2
    return half, pl.multiple_of(half * (ROWS - REACH), PAD)


def edge_kernel(
    offset_ref, pixels_ref, noise_ref, col_start_ref, col_weights_ref, row_start_ref, row_weights_ref,
    send_ref, rest_ref, edge_ref, last_weight_ref, last_patch_ref, rows_ref, rows2_ref, low_ref, low2_ref, rolled_ref,
    table_ref, flip_ref, cols_ref, cols2_ref, held_ref, held2_ref, whole_ref,
    col_first_ref, col_taps_ref, row_first_ref, row_taps_ref, sems,
):
    loads = [
        pltpu.make_async_copy(source, target, sems.at[number])
        for number, (source, target) in enumerate(
            (
                (row_start_ref, row_first_ref),
                (row_weights_ref, row_taps_ref),
                (col_start_ref, col_first_ref),
                (col_weights_ref, col_taps_ref),
                (pixels_ref, held_ref),
                (noise_ref, held2_ref),
            )
        )
    ]
    for load in loads:
        load.start()
    shift = offset_ref[0, 0]
    for load in loads[:2]:
        load.wait()
    build_rows(row_first_ref, row_taps_ref, flip_ref, rows_ref, rows2_ref)
    for load in loads[2:4]:
        load.wait()
    table_ref[...] = jnp.zeros_like(table_ref)
    for tap in range(TAPS):
        table_ref[tap : tap + 1, :] = col_taps_ref[tap]
    table_ref[TAPS : TAPS + 1, :] = col_first_ref[...].astype(F32)
    table = pltpu.roll(table_ref[...], shift, 1)
    rolled_ref[...] = table
    parts = jnp.concatenate([table[:, :EDGE], table[:, COLS - LANES :]], axis=1)
    build_cols(parts, 0, EDGE + LANES, cols_ref, cols2_ref)
    loads[4].wait()
    low_ref[...] = held_ref[...].astype(BF16)
    across = dot(low_ref[...], cols_ref[...]).astype(BF16)
    loads[5].wait()
    low2_ref[...] = held2_ref[...].astype(BF16)
    across2 = dot(low2_ref[...], cols2_ref[...]).astype(BF16)
    warped = dot(rows_ref[...], across)
    inverse = 1.0 / dot(rows2_ref[...], across2)
    scaled = warped * inverse
    mine = lax.broadcasted_iota(jnp.int32, (ROWS, EDGE), 1) >= shift
    edge_scaled = scaled[:, :EDGE]
    edge_inverse = inverse[:, :EDGE]
    edge_ref[0:ROWS, :] = edge_scaled
    edge_ref[ROWS:, :] = edge_inverse
    whole_ref[0:ROWS, :] = jnp.where(mine, 0.0, edge_scaled).astype(BF16)
    whole_ref[ROWS:, :] = jnp.where(mine, 0.0, edge_inverse).astype(BF16)
    half, start = half_start(0)
    rest = pl.multiple_of((1 - half) * REACH, PAD)
    send_ref[0:REACH, :] = whole_ref[pl.ds(start, REACH), :]
    send_ref[REACH : 2 * REACH, :] = whole_ref[pl.ds(start + ROWS, REACH), :]
    rest_ref[0 : ROWS - REACH, :] = whole_ref[pl.ds(rest, ROWS - REACH), :]
    rest_ref[ROWS - REACH :, :] = whole_ref[pl.ds(rest + ROWS, ROWS - REACH), :]
    last_inverse = inverse[:, EDGE:]
    last = scaled[:, EDGE:] / jnp.maximum(last_inverse, 0.1)
    last_weight_ref[...] = last_inverse.astype(BF16)
    last_patch_ref[...] = last.astype(BF16)
    tail = jnp.transpose(last)[LANES - 16 :].astype(BF16)
    send_ref[2 * REACH : 2 * REACH + 16, :] = tail[:, :256]
    send_ref[2 * REACH + 16 :, :] = tail[:, 256:]


def middle_kernel(
    offset_ref, coef_ref, low_ref, low2_ref, rolled_ref, rows_ref, rows2_ref,
    last_patch_ref, last_weight_ref, factors_ref, edge_ref,
    patch_ref, weight_ref, taps_ref, head_ref, sent_ref,
    cols_ref, cols2_ref,
):
    turned = jnp.concatenate(
        [jnp.transpose(edge_ref[0:ROWS, :LANES])[0:16], jnp.transpose(edge_ref[ROWS:, :LANES])[0:16]], axis=0
    )
    column = lax.broadcasted_iota(jnp.int32, (32, ROWS), 0) % 16
    head_ref[...] = jnp.where(column >= offset_ref[0, 0], turned, 0.0).astype(BF16)
    sent_ref[...] = jnp.where(column >= offset_ref[0, 0], 0.0, turned)
    width = COLS - EDGE - LANES
    build_cols(rolled_ref[...], EDGE, width, cols_ref, cols2_ref)
    across = dot(low_ref[...], cols_ref[...]).astype(BF16)
    across2 = dot(low2_ref[...], cols2_ref[...]).astype(BF16)
    warped = dot(rows_ref[...], across)
    inverse = 1.0 / dot(rows2_ref[...], across2)
    patch = (warped * inverse) / jnp.maximum(inverse, 0.1)
    weight_ref[:, :width] = inverse.astype(BF16)
    weight_ref[:, width:] = last_weight_ref[...]
    wide = jnp.concatenate([patch, last_patch_ref[...].astype(F32), jnp.zeros((ROWS, LANES), F32)], axis=1)
    patch_ref[...] = pltpu.roll(wide, RADIUS, 1).astype(BF16)
    below = lax.broadcasted_iota(jnp.int32, (LANES, LANES), 1) <= lax.broadcasted_iota(jnp.int32, (LANES, LANES), 0)
    for b, terms in enumerate(kernel_terms()):
        line = sum(coef_ref[0, k] * factors_ref[a : a + 1, :] for k, a in terms)
        line = line.astype(BF16).astype(F32)
        spread = pltpu.roll(jnp.broadcast_to(line, (LANES, LANES)), 0, 1, stride=1, stride_axis=0)
        lanes = slice(b * LANES, (b + 1) * LANES)
        taps_ref[:LANES, lanes] = jnp.where(below, spread, 0.0).astype(BF16)
        taps_ref[LANES:, lanes] = jnp.where(below, 0.0, spread).astype(BF16)


def row_block(step):
    core = lax.axis_index("visit") % 2
    return pl.multiple_of(((step + 2 * core) % 4) * LANES, LANES)


def convolve(window, taps_ref, band_ref, along_ref):
    for half in range(2):
        source = window(half)
        for piece in range(FILTERS // 2):
            lanes = slice(piece * 2 * LANES, (piece + 1) * 2 * LANES)
            along = dot(source, taps_ref[:, lanes]).astype(BF16)
            at = slice(half * LANES, (half + 1) * LANES)
            along_ref[2 * piece, PAD : PAD + ROWS, at] = along[:, :LANES]
            along_ref[2 * piece + 1, PAD : PAD + ROWS, at] = along[:, LANES:]
    for step in range(ROWS // LANES):
        at = row_block(step)
        source = jnp.concatenate([along_ref[a, pl.ds(at, WINDOW), :] for a in range(FILTERS)], axis=0)
        yield step, at, dot(band_ref[...], source)


def clear_margins(along_ref):
    for a in range(FILTERS):
        along_ref[a, 0:PAD, :] = jnp.zeros((PAD, 2 * LANES), BF16)
        along_ref[a, PAD + ROWS :, :] = jnp.zeros((PAD, 2 * LANES), BF16)


def inner_kernel(patch_ref, weight_ref, taps_ref, band_ref, matched_ref, keep_ref, give_ref, along_ref):
    clear_margins(along_ref)
    halves = (keep_ref, keep_ref, give_ref, give_ref)
    for step in range(4):
        low = LANES * (step % 2)
        halves[step][low : low + LANES, 4 * LANES :] = weight_ref[pl.ds(row_block(step), LANES), :]

    @pl.loop(0, 2)
    def _(pair):
        start = pl.multiple_of(pair * 2 * LANES, 2 * LANES)

        def window(half):
            at = pl.multiple_of(start + LANES + half * LANES, LANES)
            return patch_ref[:, pl.ds(at, 2 * LANES)]

        for step, at, matched in convolve(window, taps_ref, band_ref, along_ref):
            rows = pl.ds(at, LANES)
            matched_ref[rows, pl.ds(start, 2 * LANES)] = matched
            weight = weight_ref[rows, pl.ds(pl.multiple_of(start + LANES, LANES), 2 * LANES)].astype(F32)
            low = LANES * (step % 2)
            halves[step][low : low + LANES, pl.ds(start, 2 * LANES)] = (weight * matched).astype(BF16)


def match_half(
    side, offset_ref, scaled, weights, edge_ref, patch_ref, weight_ref, left, right, taps_ref, band_ref,
    matched_ref, term_ref, along_ref, padded_ref, held_ref,
):
    half, start = half_start(side)
    window = pl.ds(start, REACH)
    inside = pl.multiple_of(half * PAD, PAD)
    for a in range(FILTERS):
        along_ref[a, 0:PAD, :] = jnp.zeros((PAD, 2 * LANES), BF16)
        along_ref[a, REACH:, :] = jnp.zeros((PAD, 2 * LANES), BF16)
    mine = lax.broadcasted_iota(jnp.int32, (REACH, EDGE), 1) >= offset_ref[0, 0]
    total_scaled = jnp.where(mine, edge_ref[window, :], 0.0) + scaled.astype(F32)
    total_weight = jnp.where(mine, edge_ref[pl.ds(start + ROWS, REACH), :], 0.0) + weights.astype(F32)
    patch = total_scaled / jnp.maximum(total_weight, 0.1)
    held_ref[:, :EDGE] = total_weight.astype(BF16)
    held_ref[:, EDGE:] = weight_ref[window, :]
    lane = lax.broadcasted_iota(jnp.int32, (REACH, LANES), 1)
    wide = pltpu.roll(jnp.concatenate([patch, left[window, :]], axis=1), RADIUS, 1)
    padded_ref[:, :EDGE] = wide[:, :EDGE].astype(BF16)
    padded_ref[:, EDGE : EDGE + LANES] = jnp.where(
        lane < RADIUS, wide[:, EDGE:], patch_ref[window, :LANES].astype(F32)
    ).astype(BF16)
    padded_ref[:, EDGE + LANES : COLS] = patch_ref[window, LANES : COLS - EDGE]
    padded_ref[:, COLS:] = jnp.where(
        (lane >= RADIUS) & (lane < 2 * RADIUS), right[window, :],
        jnp.where(lane < RADIUS, patch_ref[window, COLS - EDGE :].astype(F32), 0.0),
    ).astype(BF16)
    own = pl.ds(inside, ROWS // 2)
    term_ref[:, 4 * LANES :] = held_ref[own, :EDGE]

    @pl.loop(0, 2)
    def _(pair):
        def place(half):
            return pl.multiple_of(jnp.where(pair == 0, half, 2 + 5 * half) * LANES, LANES)

        for number in range(2):
            source = padded_ref[:, pl.ds(place(number), 2 * LANES)]
            at = slice(number * LANES, (number + 1) * LANES)
            rows = pl.ds(pl.multiple_of(PAD - inside, PAD), REACH)
            for piece in range(FILTERS // 2):
                along = dot(source, taps_ref[:, piece * 2 * LANES : (piece + 1) * 2 * LANES]).astype(BF16)
                along_ref[2 * piece, rows, at] = along[:, :LANES]
                along_ref[2 * piece + 1, rows, at] = along[:, LANES:]
        lanes = pl.ds(pl.multiple_of(pair * 2 * LANES, LANES), 2 * LANES)
        for step in range(2):
            at = slice(step * LANES, (step + 1) * LANES)
            source = jnp.concatenate(
                [along_ref[a, step * LANES : step * LANES + WINDOW, :] for a in range(FILTERS)], axis=0
            )
            matched = dot(band_ref[...], source)
            matched_ref[at, lanes] = matched
            rows = pl.ds(pl.multiple_of(inside + step * LANES, PAD), LANES)
            weight = jnp.concatenate([held_ref[rows, pl.ds(place(number), LANES)] for number in range(2)], axis=1)
            term_ref[at, lanes] = (weight.astype(F32) * matched).astype(BF16)


def given_kernel(
    offset_ref, got_ref, ahead_ref, edge_ref, sent_ref, patch_ref, weight_ref, taps_ref, band_ref,
    matched_ref, term_ref, left_ref, right_ref,
    along_ref, padded_ref, held_ref, flip_ref,
):
    flip_ref[...] = jnp.zeros_like(flip_ref)
    flip_ref[LANES - 16 :, :256] = got_ref[2 * REACH : 2 * REACH + 16, :].astype(F32)
    flip_ref[LANES - 16 :, 256:] = got_ref[2 * REACH + 16 :, :].astype(F32)
    left_ref[...] = jnp.transpose(flip_ref[...])
    near_scaled = ahead_ref[0:16, :].astype(F32) + sent_ref[0:16, :]
    near_weight = ahead_ref[16:32, :].astype(F32) + sent_ref[16:32, :]
    flip_ref[0:16, :] = near_scaled / jnp.maximum(near_weight, 0.1)
    right_ref[...] = pltpu.roll(jnp.transpose(flip_ref[...]), RADIUS, 1)
    match_half(
        0, offset_ref, got_ref[0:REACH, :], got_ref[REACH : 2 * REACH, :], edge_ref, patch_ref, weight_ref,
        left_ref, right_ref, taps_ref, band_ref, matched_ref, term_ref, along_ref, padded_ref, held_ref,
    )


def kept_kernel(
    offset_ref, got_ref, rest_ref, edge_ref, patch_ref, weight_ref, left_ref, right_ref, taps_ref, band_ref,
    matched_ref, term_ref,
    along_ref, padded_ref, held_ref, joined_ref,
):
    half, _ = half_start(1)
    count = ROWS - REACH
    both = REACH - count
    for part in range(2):
        there = pl.multiple_of(part * REACH + half * count, PAD)
        here = pl.multiple_of(part * REACH + (1 - half) * count, PAD)
        joined_ref[pl.ds(here, both), :] = got_ref[pl.ds(there, both), :]
        here = pl.multiple_of(part * REACH + half * both, PAD)
        joined_ref[pl.ds(here, count), :] = rest_ref[part * count : (part + 1) * count, :]
    match_half(
        1, offset_ref, joined_ref[0:REACH, :], joined_ref[REACH:, :], edge_ref, patch_ref, weight_ref,
        left_ref, right_ref, taps_ref, band_ref, matched_ref, term_ref, along_ref, padded_ref, held_ref,
    )


def pair_kernel(keep_ref, got_ref, keep2_ref, got2_ref, own_ref, two_ref, one_ref, three_ref):
    chip = lax.axis_index("visit") // 2
    width = keep_ref.shape[1]
    for ahead, out_ref in ((0, own_ref), (2, two_ref), (1, one_ref), (3, three_ref)):
        rows = pl.ds(pl.multiple_of(((chip + ahead) % 4) * PIECE, PIECE), PIECE)
        first = keep_ref[rows, :].astype(F32) + got_ref[rows, :].astype(F32)
        second = keep2_ref[rows, :].astype(F32) + got2_ref[rows, :].astype(F32)
        out_ref[:, :width] = first.astype(out_ref.dtype)
        out_ref[:, width:] = second.astype(out_ref.dtype)


def coadd_kernel(own_ref, one_ref, two_ref, three_ref, coadd_ref):
    total = own_ref[...] + one_ref[...].astype(F32) + two_ref[...].astype(F32) + three_ref[...].astype(F32)
    inner, outer = total[:, : COLS + 2 * LANES], total[:, COLS + 2 * LANES :]
    weight = jnp.maximum(jnp.concatenate([outer[:, 4 * LANES :], inner[:, 4 * LANES :]], axis=1), 0.1)
    terms = jnp.concatenate([outer[:, : 3 * LANES], inner[:, : 4 * LANES], outer[:, 3 * LANES : 4 * LANES]], axis=1)
    coadd_ref[...] = (terms / weight).astype(BF16)


def final_kernel(places, *refs):
    inner_ref, *outer_refs = refs[:3]
    difference_out, image_out, difference_ref, image_ref, sems = refs[-5:]
    index = lax.axis_index("visit")
    chip, core = index // 2, index % 2
    copies = []
    for number, (side, back) in enumerate(places):
        outer_ref = outer_refs[side]
        within = pl.multiple_of(((chip + 4 - back) % 4) * PIECE, PIECE)
        rows = pl.ds(pl.multiple_of(((core + side) % 2) * (4 * PIECE) + within, PIECE), PIECE)
        near = pl.ds(within, PIECE)
        image = refs[3 + number][...].astype(F32)
        image_ref[number] = image
        difference_ref[number, :, : 3 * LANES] = outer_ref[near, : 3 * LANES] - image[:, : 3 * LANES]
        difference_ref[number, :, 3 * LANES : 7 * LANES] = inner_ref[rows, :] - image[:, 3 * LANES : 7 * LANES]
        difference_ref[number, :, 7 * LANES :] = outer_ref[near, 3 * LANES :] - image[:, 7 * LANES :]
        for which, (held, out) in enumerate(((image_ref, image_out), (difference_ref, difference_out))):
            copy = pltpu.make_async_copy(held.at[number], out.at[rows, :], sems.at[which, number])
            copy.start()
            copies.append(copy)
    for copy in copies:
        copy.wait()


def finish(places, matched, pieces, done, name, moved):
    count = len(places)
    return call(
        functools.partial(final_kernel, places),
        [((ROWS, COLS), F32), ((ROWS, COLS), F32)],
        [pltpu.VMEM((count, PIECE, COLS), F32)] * 2 + [pltpu.SemaphoreType.DMA((2, count))],
        [VMEM_SPEC] * (3 + count) + [HBM_SPEC] * len(done),
        count * PIECE * COLS,
        moved,
        name,
        HBM_SPEC,
        {3 + count + i: i for i in range(len(done))},
    )(*matched, *pieces, *done)


def call(body, outs, scratch, specs, flops, moved, name, out_spec=None, aliases=None):
    return pl.pallas_call(
        body,
        out_shape=[jax.ShapeDtypeStruct(shape, dtype) for shape, dtype in outs],
        in_specs=specs,
        out_specs=[out_spec or VMEM_SPEC for _ in outs],
        scratch_shapes=scratch,
        input_output_aliases=aliases or {},
        compiler_params=pltpu.CompilerParams(vmem_limit_bytes=VMEM_LIMIT),
        cost_estimate=pl.CostEstimate(flops=flops, bytes_accessed=moved, transcendentals=0),
        name=name,
    )


SMEM_SPEC = pl.BlockSpec(memory_space=pltpu.SMEM)
VMEM_SPEC = pl.BlockSpec(memory_space=pltpu.VMEM)
HBM_SPEC = pl.BlockSpec(memory_space=pltpu.HBM)


def shifted(x, axis, by):
    size = lax.axis_size(axis)
    return lax.ppermute(x, axis, [(i, (i + by) % size) for i in range(size)])


def in_hbm(x):
    return pltpu.with_memory_space_constraint(x, pltpu.HBM)


def partner(x):
    return lax.ppermute(x, "visit", [(i, i ^ 1) for i in range(lax.axis_size("visit"))])


def per_device(
    exposure, variance, col_start, col_weights, row_start, row_weights, offsets, basis_coef
):
    pixels = in_hbm(exposure[0])
    noise = in_hbm(variance[0])
    col_taps = in_hbm(jnp.transpose(col_weights, (1, 0, 2)))
    row_taps = in_hbm(jnp.transpose(row_weights, (1, 0, 2)))
    col_start = in_hbm(col_start)
    row_start = in_hbm(row_start)
    factors = np.zeros((16, LANES), np.float32)
    factors[:FILTERS, : 2 * RADIUS + 1] = factor_table()
    factors = np.roll(factors, -2 * RADIUS, axis=1)
    band = jnp.asarray(row_band())
    width = EDGE + LANES
    send, rest, edge, last_weight, last_patch, rows, rows2, low, low2, rolled = call(
        edge_kernel,
        [
            ((2 * REACH + 32, EDGE), BF16),
            ((2 * (ROWS - REACH), EDGE), BF16),
            ((2 * ROWS, EDGE), F32),
            ((ROWS, LANES), BF16),
            ((ROWS, LANES), BF16),
            ((ROWS, ROWS), BF16),
            ((ROWS, ROWS), BF16),
            ((ROWS, COLS), BF16),
            ((ROWS, COLS), BF16),
            ((8, COLS), F32),
        ],
        [
            pltpu.VMEM((8, COLS), F32),
            pltpu.VMEM((LANES, ROWS), F32),
            pltpu.VMEM((COLS, width), BF16),
            pltpu.VMEM((COLS, width), BF16),
            pltpu.VMEM((ROWS, COLS), F32),
            pltpu.VMEM((ROWS, COLS), F32),
            pltpu.VMEM((2 * ROWS, EDGE), BF16),
            pltpu.VMEM((1, COLS), jnp.int32),
            pltpu.VMEM((TAPS, 1, COLS), F32),
            pltpu.VMEM((1, ROWS), jnp.int32),
            pltpu.VMEM((TAPS, 1, ROWS), F32),
            pltpu.SemaphoreType.DMA((6,)),
        ],
        [SMEM_SPEC] + [HBM_SPEC] * 6,
        4 * ROWS * width * (COLS + ROWS),
        8 << 20,
        "edge_columns",
    )(offsets, pixels, noise, col_start, col_taps, row_start, row_taps)
    got = shifted(send, "patch", 1)
    got_rest = shifted(rest, "patch", 1)
    width = COLS - EDGE - LANES
    patch, weight, taps, head, sent = call(
        middle_kernel,
        [
            ((ROWS, COLS - EDGE + LANES), BF16),
            ((ROWS, COLS - EDGE), BF16),
            ((2 * LANES, FILTERS * LANES), BF16),
            ((32, ROWS), BF16),
            ((32, ROWS), F32),
        ],
        [pltpu.VMEM((COLS, width), BF16), pltpu.VMEM((COLS, width), BF16)],
        [SMEM_SPEC] * 2 + [VMEM_SPEC] * 9,
        1 << 20,
        1 << 10,
        "middle_columns",
    )(offsets, basis_coef, low, low2, rolled, rows, rows2, last_patch, last_weight, jnp.asarray(factors), edge)
    ahead = shifted(head, "patch", -1)
    conv_flops = 2 * ROWS * ROWS * FILTERS * (2 * LANES + WINDOW)
    inner_width = COLS + 2 * LANES
    inner, keep, give = call(
        inner_kernel,
        [((ROWS, 4 * LANES), F32), ((ROWS // 2, inner_width), BF16), ((ROWS // 2, inner_width), BF16)],
        [pltpu.VMEM((FILTERS, ROWS + 2 * PAD, 2 * LANES), BF16)],
        [VMEM_SPEC] * 4,
        1 << 20,
        1 << 10,
        "inner_match",
    )(patch, weight, taps, band)
    inner_sum = keep, partner(give)
    outer_width = 4 * LANES + EDGE
    half_outs = [((ROWS // 2, 4 * LANES), F32), ((ROWS // 2, outer_width), BF16)]
    half_scratch = [
        pltpu.VMEM((FILTERS, REACH + PAD, 2 * LANES), BF16),
        pltpu.VMEM((REACH, COLS + LANES), BF16),
        pltpu.VMEM((REACH, COLS), BF16),
    ]
    given, give, left, right = call(
        given_kernel,
        half_outs + [((ROWS, LANES), F32)] * 2,
        half_scratch + [pltpu.VMEM((LANES, ROWS), F32)],
        [SMEM_SPEC] + [VMEM_SPEC] * 8,
        1 << 20,
        1 << 10,
        "given_match",
    )(offsets, got, ahead, edge, sent, patch, weight, taps, band)
    kept, keep = call(
        kept_kernel,
        half_outs,
        half_scratch + [pltpu.VMEM((2 * REACH, EDGE), BF16)],
        [SMEM_SPEC] + [VMEM_SPEC] * 9,
        8 * conv_flops,
        64 << 20,
        "kept_match",
    )(offsets, got, got_rest, edge, patch, weight, left, right, taps, band)
    own_piece, *others = call(
        pair_kernel,
        [((PIECE, inner_width + outer_width), F32)] + [((PIECE, inner_width + outer_width), BF16)] * 3,
        [],
        [VMEM_SPEC] * 4,
        ROWS * COLS,
        3 << 20,
        "pair_sum",
    )(*inner_sum, keep, partner(give))
    others = [shifted(x, "visit", 2 * ahead) for ahead, x in zip((2, 1, 3), others)]
    (piece,) = call(
        coadd_kernel, [((PIECE, COLS), BF16)], [], [VMEM_SPEC] * 4, 8 * PIECE * COLS, 2 << 20, "coadd"
    )(own_piece, *others)
    backs = (1, 3, 2)
    column = [shifted(piece, "visit", 2 * ahead) for ahead in backs]
    matched = inner, kept, given
    across = partner(piece)
    done = finish(((0, 0), (1, 0)), matched, [piece, across], [], "difference_near", 1 << 20)
    *done, column[2] = lax.optimization_barrier((*done, column[2]))
    swapped = [partner(x) for x in column]
    done = finish(tuple((0, back) for back in backs), matched, column, done, "difference_own", 64 << 20)
    difference, image = finish(tuple((1, back) for back in backs), matched, swapped, done, "difference_other", 3 << 20)
    return (difference[None], image)


def solution(mesh):
    return jax.shard_map(
        per_device,
        mesh=mesh,
        in_specs=(
            P("visit", None, "patch"),
            P("visit", None, "patch"),
            P("visit", "patch"),
            P("visit", None, "patch"),
            P("visit", "patch"),
            P("visit", None, "patch"),
            P("visit", "patch"),
            P("visit", None),
        ),
        out_specs=(P("visit", None, "patch"), P(None, "patch")),
        check_vma=False,
    )
```

```python
import functools
import math

import jax
import jax.numpy as jnp
import numpy as np
from jax import lax
from jax.experimental import pallas as pl
from jax.experimental.pallas import tpu as pltpu
from jax.sharding import PartitionSpec as P

RADIUS = 10
TAPS = 6
ROWS = 512
COLS = 1024
EDGE = 256
LANES = 128
FILTERS = 12
WINDOW = 160
PAD = 16
REACH = 272
PIECE = 64
SPREADS = (0.7, 1.5, 3.0)
DEGREES = (4, 3, 2)
F32 = jnp.float32
BF16 = jnp.bfloat16
VMEM_LIMIT = 28 * 1024 * 1024


def factor_table():
    distance = np.arange(2 * RADIUS + 1).astype(np.float32) - RADIUS
    rows = []
    for spread, degree in zip(SPREADS, DEGREES):
        gaussian = np.exp(-distance * distance / np.float32(2.0 * spread * spread)) / np.float32(
            spread * math.sqrt(2.0 * math.pi)
        )
        for exponent in range(degree + 1):
            rows.append(gaussian * (distance / np.float32(spread)) ** exponent)
    return np.stack(rows).astype(np.float32)


def kernel_terms():
    terms = [[] for _ in range(FILTERS)]
    kernel = 0
    first = 0
    for degree in DEGREES:
        for i in range(degree + 1):
            for j in range(degree + 1 - i):
                terms[first + j].append((kernel, first + i))
                kernel += 1
        first += degree + 1
    return terms


def row_band():
    factors = factor_table().astype(BF16)
    gap = np.arange(LANES)[:, None] + PAD - np.arange(WINDOW)[None, :]
    inside = np.abs(gap) <= RADIUS
    at = np.clip(gap + RADIUS, 0, 2 * RADIUS)
    band = np.where(inside[None], factors[:, at], np.zeros((), BF16))
    return band.transpose(1, 0, 2).reshape(LANES, FILTERS * WINDOW).astype(BF16)


def dot(a, b):
    return jnp.dot(a, b, preferred_element_type=F32)


def nth_tap(gap):
    return jnp.where((gap & -8) == 0, gap, 7)


def build_cols(table, low, width, cols_ref, square_ref):
    taps = table[:, low : low + width]
    first = taps[TAPS : TAPS + 1].astype(jnp.int32)
    taps = jnp.where(lax.broadcasted_iota(jnp.int32, (8, width), 0) < TAPS, taps, 0.0)
    base = lax.broadcasted_iota(jnp.int32, (8, width), 0) - first

    @pl.loop(0, COLS // LANES)
    def _(block):
        for group in range(LANES // PAD):
            at = block * LANES + group * PAD
            value = jnp.concatenate(
                [jnp.take_along_axis(taps, nth_tap(base + (at + step)), axis=0) for step in (0, 8)], axis=0
            )
            rows = pl.ds(pl.multiple_of(at, PAD), PAD)
            cols_ref[rows, :] = value.astype(BF16)
            square_ref[rows, :] = (value * value).astype(BF16)


def build_rows(row_start_ref, row_weights_ref, flip_ref, rows_ref, square_ref):
    flip_ref[...] = jnp.zeros_like(flip_ref)
    for tap in range(TAPS):
        flip_ref[tap : tap + 1, :] = row_weights_ref[tap]
    flip_ref[8:9, :] = row_start_ref[...].astype(F32)
    for block in range(ROWS // LANES):
        at = slice(block * LANES, (block + 1) * LANES)
        turned = jnp.transpose(flip_ref[:, at])
        lane = lax.broadcasted_iota(jnp.int32, (LANES, LANES), 1)
        base = lane - turned[:, 8:9].astype(jnp.int32)
        for part in range(ROWS // LANES):
            value = jnp.take_along_axis(turned, nth_tap(base + part * LANES), axis=1)
            lanes = slice(part * LANES, (part + 1) * LANES)
            rows_ref[at, lanes] = value.astype(BF16)
            square_ref[at, lanes] = (value * value).astype(BF16)


def half_start(side):
    core = lax.axis_index("visit") % 2
    half = (core + 1 - side) % 2
    return half, pl.multiple_of(half * (ROWS - REACH), PAD)


def edge_kernel(
    offset_ref, pixels_ref, noise_ref, col_start_ref, col_weights_ref, row_start_ref, row_weights_ref,
    send_ref, rest_ref, edge_ref, last_weight_ref, last_patch_ref, rows_ref, rows2_ref, low_ref, low2_ref, rolled_ref,
    table_ref, flip_ref, cols_ref, cols2_ref, held_ref, held2_ref, whole_ref,
    col_first_ref, col_taps_ref, row_first_ref, row_taps_ref, sems,
):
    loads = [
        pltpu.make_async_copy(source, target, sems.at[number])
        for number, (source, target) in enumerate(
            (
                (row_start_ref, row_first_ref),
                (row_weights_ref, row_taps_ref),
                (col_start_ref, col_first_ref),
                (col_weights_ref, col_taps_ref),
                (pixels_ref, held_ref),
                (noise_ref, held2_ref),
            )
        )
    ]
    for load in loads:
        load.start()
    shift = offset_ref[0, 0]
    for load in loads[:2]:
        load.wait()
    build_rows(row_first_ref, row_taps_ref, flip_ref, rows_ref, rows2_ref)
    for load in loads[2:4]:
        load.wait()
    table_ref[...] = jnp.zeros_like(table_ref)
    for tap in range(TAPS):
        table_ref[tap : tap + 1, :] = col_taps_ref[tap]
    table_ref[TAPS : TAPS + 1, :] = col_first_ref[...].astype(F32)
    table = pltpu.roll(table_ref[...], shift, 1)
    rolled_ref[...] = table
    parts = jnp.concatenate([table[:, :EDGE], table[:, COLS - LANES :]], axis=1)
    build_cols(parts, 0, EDGE + LANES, cols_ref, cols2_ref)
    loads[4].wait()
    low_ref[...] = held_ref[...].astype(BF16)
    across = dot(low_ref[...], cols_ref[...]).astype(BF16)
    loads[5].wait()
    low2_ref[...] = held2_ref[...].astype(BF16)
    across2 = dot(low2_ref[...], cols2_ref[...]).astype(BF16)
    warped = dot(rows_ref[...], across)
    inverse = 1.0 / dot(rows2_ref[...], across2)
    scaled = warped * inverse
    mine = lax.broadcasted_iota(jnp.int32, (ROWS, EDGE), 1) >= shift
    edge_scaled = scaled[:, :EDGE]
    edge_inverse = inverse[:, :EDGE]
    edge_ref[0:ROWS, :] = edge_scaled
    edge_ref[ROWS:, :] = edge_inverse
    whole_ref[0:ROWS, :] = jnp.where(mine, 0.0, edge_scaled).astype(BF16)
    whole_ref[ROWS:, :] = jnp.where(mine, 0.0, edge_inverse).astype(BF16)
    half, start = half_start(0)
    rest = pl.multiple_of((1 - half) * REACH, PAD)
    send_ref[0:REACH, :] = whole_ref[pl.ds(start, REACH), :]
    send_ref[REACH : 2 * REACH, :] = whole_ref[pl.ds(start + ROWS, REACH), :]
    rest_ref[0 : ROWS - REACH, :] = whole_ref[pl.ds(rest, ROWS - REACH), :]
    rest_ref[ROWS - REACH :, :] = whole_ref[pl.ds(rest + ROWS, ROWS - REACH), :]
    last_inverse = inverse[:, EDGE:]
    last = scaled[:, EDGE:] / jnp.maximum(last_inverse, 0.1)
    last_weight_ref[...] = last_inverse.astype(BF16)
    last_patch_ref[...] = last.astype(BF16)
    tail = jnp.transpose(last)[LANES - 16 :].astype(BF16)
    send_ref[2 * REACH : 2 * REACH + 16, :] = tail[:, :256]
    send_ref[2 * REACH + 16 :, :] = tail[:, 256:]


def middle_kernel(
    offset_ref, coef_ref, low_ref, low2_ref, rolled_ref, rows_ref, rows2_ref,
    last_patch_ref, last_weight_ref, factors_ref, edge_ref,
    patch_ref, weight_ref, taps_ref, head_ref, sent_ref,
    cols_ref, cols2_ref,
):
    turned = jnp.concatenate(
        [jnp.transpose(edge_ref[0:ROWS, :LANES])[0:16], jnp.transpose(edge_ref[ROWS:, :LANES])[0:16]], axis=0
    )
    column = lax.broadcasted_iota(jnp.int32, (32, ROWS), 0) % 16
    head_ref[...] = jnp.where(column >= offset_ref[0, 0], turned, 0.0).astype(BF16)
    sent_ref[...] = jnp.where(column >= offset_ref[0, 0], 0.0, turned)
    width = COLS - EDGE - LANES
    build_cols(rolled_ref[...], EDGE, width, cols_ref, cols2_ref)
    across = dot(low_ref[...], cols_ref[...]).astype(BF16)
    across2 = dot(low2_ref[...], cols2_ref[...]).astype(BF16)
    warped = dot(rows_ref[...], across)
    inverse = 1.0 / dot(rows2_ref[...], across2)
    patch = (warped * inverse) / jnp.maximum(inverse, 0.1)
    weight_ref[:, :width] = inverse.astype(BF16)
    weight_ref[:, width:] = last_weight_ref[...]
    wide = jnp.concatenate([patch, last_patch_ref[...].astype(F32), jnp.zeros((ROWS, LANES), F32)], axis=1)
    patch_ref[...] = pltpu.roll(wide, RADIUS, 1).astype(BF16)
    below = lax.broadcasted_iota(jnp.int32, (LANES, LANES), 1) <= lax.broadcasted_iota(jnp.int32, (LANES, LANES), 0)
    for b, terms in enumerate(kernel_terms()):
        line = sum(coef_ref[0, k] * factors_ref[a : a + 1, :] for k, a in terms)
        line = line.astype(BF16).astype(F32)
        spread = pltpu.roll(jnp.broadcast_to(line, (LANES, LANES)), 0, 1, stride=1, stride_axis=0)
        lanes = slice(b * LANES, (b + 1) * LANES)
        taps_ref[:LANES, lanes] = jnp.where(below, spread, 0.0).astype(BF16)
        taps_ref[LANES:, lanes] = jnp.where(below, 0.0, spread).astype(BF16)


def row_block(step):
    core = lax.axis_index("visit") % 2
    return pl.multiple_of(((step + 2 * core) % 4) * LANES, LANES)


def convolve(window, taps_ref, band_ref, along_ref):
    for half in range(2):
        source = window(half)
        for piece in range(FILTERS // 2):
            lanes = slice(piece * 2 * LANES, (piece + 1) * 2 * LANES)
            along = dot(source, taps_ref[:, lanes]).astype(BF16)
            at = slice(half * LANES, (half + 1) * LANES)
            along_ref[2 * piece, PAD : PAD + ROWS, at] = along[:, :LANES]
            along_ref[2 * piece + 1, PAD : PAD + ROWS, at] = along[:, LANES:]
    for step in range(ROWS // LANES):
        at = row_block(step)
        source = jnp.concatenate([along_ref[a, pl.ds(at, WINDOW), :] for a in range(FILTERS)], axis=0)
        yield step, at, dot(band_ref[...], source)


def clear_margins(along_ref):
    for a in range(FILTERS):
        along_ref[a, 0:PAD, :] = jnp.zeros((PAD, 2 * LANES), BF16)
        along_ref[a, PAD + ROWS :, :] = jnp.zeros((PAD, 2 * LANES), BF16)


def inner_kernel(patch_ref, weight_ref, taps_ref, band_ref, matched_ref, keep_ref, give_ref, along_ref):
    clear_margins(along_ref)
    halves = (keep_ref, keep_ref, give_ref, give_ref)
    for step in range(4):
        low = LANES * (step % 2)
        halves[step][low : low + LANES, 4 * LANES :] = weight_ref[pl.ds(row_block(step), LANES), :]

    @pl.loop(0, 2)
    def _(pair):
        start = pl.multiple_of(pair * 2 * LANES, 2 * LANES)

        def window(half):
            at = pl.multiple_of(start + LANES + half * LANES, LANES)
            return patch_ref[:, pl.ds(at, 2 * LANES)]

        for step, at, matched in convolve(window, taps_ref, band_ref, along_ref):
            rows = pl.ds(at, LANES)
            matched_ref[rows, pl.ds(start, 2 * LANES)] = matched
            weight = weight_ref[rows, pl.ds(pl.multiple_of(start + LANES, LANES), 2 * LANES)].astype(F32)
            low = LANES * (step % 2)
            halves[step][low : low + LANES, pl.ds(start, 2 * LANES)] = (weight * matched).astype(BF16)


def match_half(
    side, offset_ref, scaled, weights, edge_ref, patch_ref, weight_ref, left, right, taps_ref, band_ref,
    matched_ref, term_ref, along_ref, padded_ref, held_ref,
):
    half, start = half_start(side)
    window = pl.ds(start, REACH)
    inside = pl.multiple_of(half * PAD, PAD)
    for a in range(FILTERS):
        along_ref[a, 0:PAD, :] = jnp.zeros((PAD, 2 * LANES), BF16)
        along_ref[a, REACH:, :] = jnp.zeros((PAD, 2 * LANES), BF16)
    mine = lax.broadcasted_iota(jnp.int32, (REACH, EDGE), 1) >= offset_ref[0, 0]
    total_scaled = jnp.where(mine, edge_ref[window, :], 0.0) + scaled.astype(F32)
    total_weight = jnp.where(mine, edge_ref[pl.ds(start + ROWS, REACH), :], 0.0) + weights.astype(F32)
    patch = total_scaled / jnp.maximum(total_weight, 0.1)
    held_ref[:, :EDGE] = total_weight.astype(BF16)
    held_ref[:, EDGE:] = weight_ref[window, :]
    lane = lax.broadcasted_iota(jnp.int32, (REACH, LANES), 1)
    wide = pltpu.roll(jnp.concatenate([patch, left[window, :]], axis=1), RADIUS, 1)
    padded_ref[:, :EDGE] = wide[:, :EDGE].astype(BF16)
    padded_ref[:, EDGE : EDGE + LANES] = jnp.where(
        lane < RADIUS, wide[:, EDGE:], patch_ref[window, :LANES].astype(F32)
    ).astype(BF16)
    padded_ref[:, EDGE + LANES : COLS] = patch_ref[window, LANES : COLS - EDGE]
    padded_ref[:, COLS:] = jnp.where(
        (lane >= RADIUS) & (lane < 2 * RADIUS), right[window, :],
        jnp.where(lane < RADIUS, patch_ref[window, COLS - EDGE :].astype(F32), 0.0),
    ).astype(BF16)
    own = pl.ds(inside, ROWS // 2)
    term_ref[:, 4 * LANES :] = held_ref[own, :EDGE]

    @pl.loop(0, 2)
    def _(pair):
        def place(half):
            return pl.multiple_of(jnp.where(pair == 0, half, 2 + 5 * half) * LANES, LANES)

        for number in range(2):
            source = padded_ref[:, pl.ds(place(number), 2 * LANES)]
            at = slice(number * LANES, (number + 1) * LANES)
            rows = pl.ds(pl.multiple_of(PAD - inside, PAD), REACH)
            for piece in range(FILTERS // 2):
                along = dot(source, taps_ref[:, piece * 2 * LANES : (piece + 1) * 2 * LANES]).astype(BF16)
                along_ref[2 * piece, rows, at] = along[:, :LANES]
                along_ref[2 * piece + 1, rows, at] = along[:, LANES:]
        lanes = pl.ds(pl.multiple_of(pair * 2 * LANES, LANES), 2 * LANES)
        for step in range(2):
            at = slice(step * LANES, (step + 1) * LANES)
            source = jnp.concatenate(
                [along_ref[a, step * LANES : step * LANES + WINDOW, :] for a in range(FILTERS)], axis=0
            )
            matched = dot(band_ref[...], source)
            matched_ref[at, lanes] = matched
            rows = pl.ds(pl.multiple_of(inside + step * LANES, PAD), LANES)
            weight = jnp.concatenate([held_ref[rows, pl.ds(place(number), LANES)] for number in range(2)], axis=1)
            term_ref[at, lanes] = (weight.astype(F32) * matched).astype(BF16)


def given_kernel(
    offset_ref, got_ref, ahead_ref, edge_ref, sent_ref, patch_ref, weight_ref, taps_ref, band_ref,
    matched_ref, term_ref, left_ref, right_ref,
    along_ref, padded_ref, held_ref, flip_ref,
):
    flip_ref[...] = jnp.zeros_like(flip_ref)
    flip_ref[LANES - 16 :, :256] = got_ref[2 * REACH : 2 * REACH + 16, :].astype(F32)
    flip_ref[LANES - 16 :, 256:] = got_ref[2 * REACH + 16 :, :].astype(F32)
    left_ref[...] = jnp.transpose(flip_ref[...])
    near_scaled = ahead_ref[0:16, :].astype(F32) + sent_ref[0:16, :]
    near_weight = ahead_ref[16:32, :].astype(F32) + sent_ref[16:32, :]
    flip_ref[0:16, :] = near_scaled / jnp.maximum(near_weight, 0.1)
    right_ref[...] = pltpu.roll(jnp.transpose(flip_ref[...]), RADIUS, 1)
    match_half(
        0, offset_ref, got_ref[0:REACH, :], got_ref[REACH : 2 * REACH, :], edge_ref, patch_ref, weight_ref,
        left_ref, right_ref, taps_ref, band_ref, matched_ref, term_ref, along_ref, padded_ref, held_ref,
    )


def kept_kernel(
    offset_ref, got_ref, rest_ref, edge_ref, patch_ref, weight_ref, left_ref, right_ref, taps_ref, band_ref,
    matched_ref, term_ref,
    along_ref, padded_ref, held_ref, joined_ref,
):
    half, _ = half_start(1)
    count = ROWS - REACH
    both = REACH - count
    for part in range(2):
        there = pl.multiple_of(part * REACH + half * count, PAD)
        here = pl.multiple_of(part * REACH + (1 - half) * count, PAD)
        joined_ref[pl.ds(here, both), :] = got_ref[pl.ds(there, both), :]
        here = pl.multiple_of(part * REACH + half * both, PAD)
        joined_ref[pl.ds(here, count), :] = rest_ref[part * count : (part + 1) * count, :]
    match_half(
        1, offset_ref, joined_ref[0:REACH, :], joined_ref[REACH:, :], edge_ref, patch_ref, weight_ref,
        left_ref, right_ref, taps_ref, band_ref, matched_ref, term_ref, along_ref, padded_ref, held_ref,
    )


def pair_kernel(keep_ref, got_ref, keep2_ref, got2_ref, own_ref, two_ref, one_ref, three_ref):
    chip = lax.axis_index("visit") // 2
    width = keep_ref.shape[1]
    for ahead, out_ref in ((0, own_ref), (2, two_ref), (1, one_ref), (3, three_ref)):
        rows = pl.ds(pl.multiple_of(((chip + ahead) % 4) * PIECE, PIECE), PIECE)
        first = keep_ref[rows, :].astype(F32) + got_ref[rows, :].astype(F32)
        second = keep2_ref[rows, :].astype(F32) + got2_ref[rows, :].astype(F32)
        out_ref[:, :width] = first.astype(out_ref.dtype)
        out_ref[:, width:] = second.astype(out_ref.dtype)


def coadd_kernel(own_ref, one_ref, two_ref, three_ref, coadd_ref):
    total = own_ref[...] + one_ref[...].astype(F32) + two_ref[...].astype(F32) + three_ref[...].astype(F32)
    inner, outer = total[:, : COLS + 2 * LANES], total[:, COLS + 2 * LANES :]
    weight = jnp.maximum(jnp.concatenate([outer[:, 4 * LANES :], inner[:, 4 * LANES :]], axis=1), 0.1)
    terms = jnp.concatenate([outer[:, : 3 * LANES], inner[:, : 4 * LANES], outer[:, 3 * LANES : 4 * LANES]], axis=1)
    coadd_ref[...] = (terms / weight).astype(BF16)


def final_kernel(places, *refs):
    inner_ref, *outer_refs = refs[:3]
    difference_out, image_out, difference_ref, image_ref, sems = refs[-5:]
    index = lax.axis_index("visit")
    chip, core = index // 2, index % 2
    copies = []
    for number, (side, back) in enumerate(places):
        outer_ref = outer_refs[side]
        within = pl.multiple_of(((chip + 4 - back) % 4) * PIECE, PIECE)
        rows = pl.ds(pl.multiple_of(((core + side) % 2) * (4 * PIECE) + within, PIECE), PIECE)
        near = pl.ds(within, PIECE)
        image = refs[3 + number][...].astype(F32)
        image_ref[number] = image
        difference_ref[number, :, : 3 * LANES] = outer_ref[near, : 3 * LANES] - image[:, : 3 * LANES]
        difference_ref[number, :, 3 * LANES : 7 * LANES] = inner_ref[rows, :] - image[:, 3 * LANES : 7 * LANES]
        difference_ref[number, :, 7 * LANES :] = outer_ref[near, 3 * LANES :] - image[:, 7 * LANES :]
        for which, (held, out) in enumerate(((image_ref, image_out), (difference_ref, difference_out))):
            copy = pltpu.make_async_copy(held.at[number], out.at[rows, :], sems.at[which, number])
            copy.start()
            copies.append(copy)
    for copy in copies:
        copy.wait()


def finish(places, matched, pieces, done, name, moved):
    count = len(places)
    return call(
        functools.partial(final_kernel, places),
        [((ROWS, COLS), F32), ((ROWS, COLS), F32)],
        [pltpu.VMEM((count, PIECE, COLS), F32)] * 2 + [pltpu.SemaphoreType.DMA((2, count))],
        [VMEM_SPEC] * (3 + count) + [HBM_SPEC] * len(done),
        count * PIECE * COLS,
        moved,
        name,
        HBM_SPEC,
        {3 + count + i: i for i in range(len(done))},
    )(*matched, *pieces, *done)


def call(body, outs, scratch, specs, flops, moved, name, out_spec=None, aliases=None):
    return pl.pallas_call(
        body,
        out_shape=[jax.ShapeDtypeStruct(shape, dtype) for shape, dtype in outs],
        in_specs=specs,
        out_specs=[out_spec or VMEM_SPEC for _ in outs],
        scratch_shapes=scratch,
        input_output_aliases=aliases or {},
        compiler_params=pltpu.CompilerParams(vmem_limit_bytes=VMEM_LIMIT),
        cost_estimate=pl.CostEstimate(flops=flops, bytes_accessed=moved, transcendentals=0),
        name=name,
    )


SMEM_SPEC = pl.BlockSpec(memory_space=pltpu.SMEM)
VMEM_SPEC = pl.BlockSpec(memory_space=pltpu.VMEM)
HBM_SPEC = pl.BlockSpec(memory_space=pltpu.HBM)


def shifted(x, axis, by):
    size = lax.axis_size(axis)
    return lax.ppermute(x, axis, [(i, (i + by) % size) for i in range(size)])


def in_hbm(x):
    return pltpu.with_memory_space_constraint(x, pltpu.HBM)


def partner(x):
    return lax.ppermute(x, "visit", [(i, i ^ 1) for i in range(lax.axis_size("visit"))])


def per_device(
    exposure, variance, col_start, col_weights, row_start, row_weights, offsets, basis_coef
):
    pixels = in_hbm(exposure[0])
    noise = in_hbm(variance[0])
    col_taps = in_hbm(jnp.transpose(col_weights, (1, 0, 2)))
    row_taps = in_hbm(jnp.transpose(row_weights, (1, 0, 2)))
    col_start = in_hbm(col_start)
    row_start = in_hbm(row_start)
    factors = np.zeros((16, LANES), np.float32)
    factors[:FILTERS, : 2 * RADIUS + 1] = factor_table()
    factors = np.roll(factors, -2 * RADIUS, axis=1)
    band = jnp.asarray(row_band())
    width = EDGE + LANES
    send, rest, edge, last_weight, last_patch, rows, rows2, low, low2, rolled = call(
        edge_kernel,
        [
            ((2 * REACH + 32, EDGE), BF16),
            ((2 * (ROWS - REACH), EDGE), BF16),
            ((2 * ROWS, EDGE), F32),
            ((ROWS, LANES), BF16),
            ((ROWS, LANES), BF16),
            ((ROWS, ROWS), BF16),
            ((ROWS, ROWS), BF16),
            ((ROWS, COLS), BF16),
            ((ROWS, COLS), BF16),
            ((8, COLS), F32),
        ],
        [
            pltpu.VMEM((8, COLS), F32),
            pltpu.VMEM((LANES, ROWS), F32),
            pltpu.VMEM((COLS, width), BF16),
            pltpu.VMEM((COLS, width), BF16),
            pltpu.VMEM((ROWS, COLS), F32),
            pltpu.VMEM((ROWS, COLS), F32),
            pltpu.VMEM((2 * ROWS, EDGE), BF16),
            pltpu.VMEM((1, COLS), jnp.int32),
            pltpu.VMEM((TAPS, 1, COLS), F32),
            pltpu.VMEM((1, ROWS), jnp.int32),
            pltpu.VMEM((TAPS, 1, ROWS), F32),
            pltpu.SemaphoreType.DMA((6,)),
        ],
        [SMEM_SPEC] + [HBM_SPEC] * 6,
        4 * ROWS * width * (COLS + ROWS),
        8 << 20,
        "edge_columns",
    )(offsets, pixels, noise, col_start, col_taps, row_start, row_taps)
    got = shifted(send, "patch", 1)
    got_rest = shifted(rest, "patch", 1)
    width = COLS - EDGE - LANES
    patch, weight, taps, head, sent = call(
        middle_kernel,
        [
            ((ROWS, COLS - EDGE + LANES), BF16),
            ((ROWS, COLS - EDGE), BF16),
            ((2 * LANES, FILTERS * LANES), BF16),
            ((32, ROWS), BF16),
            ((32, ROWS), F32),
        ],
        [pltpu.VMEM((COLS, width), BF16), pltpu.VMEM((COLS, width), BF16)],
        [SMEM_SPEC] * 2 + [VMEM_SPEC] * 9,
        1 << 20,
        1 << 10,
        "middle_columns",
    )(offsets, basis_coef, low, low2, rolled, rows, rows2, last_patch, last_weight, jnp.asarray(factors), edge)
    ahead = shifted(head, "patch", -1)
    conv_flops = 2 * ROWS * ROWS * FILTERS * (2 * LANES + WINDOW)
    inner_width = COLS + 2 * LANES
    inner, keep, give = call(
        inner_kernel,
        [((ROWS, 4 * LANES), F32), ((ROWS // 2, inner_width), BF16), ((ROWS // 2, inner_width), BF16)],
        [pltpu.VMEM((FILTERS, ROWS + 2 * PAD, 2 * LANES), BF16)],
        [VMEM_SPEC] * 4,
        1 << 20,
        1 << 10,
        "inner_match",
    )(patch, weight, taps, band)
    inner_sum = keep, partner(give)
    outer_width = 4 * LANES + EDGE
    half_outs = [((ROWS // 2, 4 * LANES), F32), ((ROWS // 2, outer_width), BF16)]
    half_scratch = [
        pltpu.VMEM((FILTERS, REACH + PAD, 2 * LANES), BF16),
        pltpu.VMEM((REACH, COLS + LANES), BF16),
        pltpu.VMEM((REACH, COLS), BF16),
    ]
    given, give, left, right = call(
        given_kernel,
        half_outs + [((ROWS, LANES), F32)] * 2,
        half_scratch + [pltpu.VMEM((LANES, ROWS), F32)],
        [SMEM_SPEC] + [VMEM_SPEC] * 8,
        1 << 20,
        1 << 10,
        "given_match",
    )(offsets, got, ahead, edge, sent, patch, weight, taps, band)
    kept, keep = call(
        kept_kernel,
        half_outs,
        half_scratch + [pltpu.VMEM((2 * REACH, EDGE), BF16)],
        [SMEM_SPEC] + [VMEM_SPEC] * 9,
        8 * conv_flops,
        64 << 20,
        "kept_match",
    )(offsets, got, got_rest, edge, patch, weight, left, right, taps, band)
    own_piece, *others = call(
        pair_kernel,
        [((PIECE, inner_width + outer_width), F32)] + [((PIECE, inner_width + outer_width), BF16)] * 3,
        [],
        [VMEM_SPEC] * 4,
        ROWS * COLS,
        3 << 20,
        "pair_sum",
    )(*inner_sum, keep, partner(give))
    others = [shifted(x, "visit", 2 * ahead) for ahead, x in zip((2, 1, 3), others)]
    (piece,) = call(
        coadd_kernel, [((PIECE, COLS), BF16)], [], [VMEM_SPEC] * 4, 8 * PIECE * COLS, 2 << 20, "coadd"
    )(own_piece, *others)
    backs = (1, 3, 2)
    column = [shifted(piece, "visit", 2 * ahead) for ahead in backs]
    matched = inner, kept, given
    done = finish(((0, 0),), matched, [piece], [], "difference_near", 1 << 20)
    *done, column[2] = lax.optimization_barrier((*done, column[2]))
    swapped = [partner(x) for x in [piece, *column]]
    done = finish(tuple((0, back) for back in backs), matched, column, done, "difference_own", 64 << 20)
    difference, image = finish(tuple((1, back) for back in (0, *backs)), matched, swapped, done, "difference_other", 3 << 20)
    return (difference[None], image)


def solution(mesh):
    return jax.shard_map(
        per_device,
        mesh=mesh,
        in_specs=(
            P("visit", None, "patch"),
            P("visit", None, "patch"),
            P("visit", "patch"),
            P("visit", None, "patch"),
            P("visit", "patch"),
            P("visit", None, "patch"),
            P("visit", "patch"),
            P("visit", None),
        ),
        out_specs=(P("visit", None, "patch"), P(None, "patch")),
        check_vma=False,
    )
```

```python
import functools
import math

import jax
import jax.numpy as jnp
import numpy as np
from jax import lax
from jax.experimental import pallas as pl
from jax.experimental.pallas import tpu as pltpu
from jax.sharding import PartitionSpec as P

RADIUS = 10
TAPS = 6
ROWS = 512
COLS = 1024
EDGE = 256
LANES = 128
FILTERS = 12
WINDOW = 160
PAD = 16
REACH = 272
PIECE = 64
SPREADS = (0.7, 1.5, 3.0)
DEGREES = (4, 3, 2)
F32 = jnp.float32
BF16 = jnp.bfloat16
VMEM_LIMIT = 28 * 1024 * 1024


def factor_table():
    distance = np.arange(2 * RADIUS + 1).astype(np.float32) - RADIUS
    rows = []
    for spread, degree in zip(SPREADS, DEGREES):
        gaussian = np.exp(-distance * distance / np.float32(2.0 * spread * spread)) / np.float32(
            spread * math.sqrt(2.0 * math.pi)
        )
        for exponent in range(degree + 1):
            rows.append(gaussian * (distance / np.float32(spread)) ** exponent)
    return np.stack(rows).astype(np.float32)


def kernel_terms():
    terms = [[] for _ in range(FILTERS)]
    kernel = 0
    first = 0
    for degree in DEGREES:
        for i in range(degree + 1):
            for j in range(degree + 1 - i):
                terms[first + j].append((kernel, first + i))
                kernel += 1
        first += degree + 1
    return terms


def row_band():
    factors = factor_table().astype(BF16)
    gap = np.arange(LANES)[:, None] + PAD - np.arange(WINDOW)[None, :]
    inside = np.abs(gap) <= RADIUS
    at = np.clip(gap + RADIUS, 0, 2 * RADIUS)
    band = np.where(inside[None], factors[:, at], np.zeros((), BF16))
    return band.transpose(1, 0, 2).reshape(LANES, FILTERS * WINDOW).astype(BF16)


def dot(a, b):
    return jnp.dot(a, b, preferred_element_type=F32)


def nth_tap(gap):
    return jnp.where((gap & -8) == 0, gap, 7)


def build_cols(table, low, width, cols_ref, square_ref):
    taps = table[:, low : low + width]
    first = taps[TAPS : TAPS + 1].astype(jnp.int32)
    taps = jnp.where(lax.broadcasted_iota(jnp.int32, (8, width), 0) < TAPS, taps, 0.0)
    base = lax.broadcasted_iota(jnp.int32, (8, width), 0) - first

    @pl.loop(0, COLS // LANES)
    def _(block):
        for group in range(LANES // PAD):
            at = block * LANES + group * PAD
            value = jnp.concatenate(
                [jnp.take_along_axis(taps, nth_tap(base + (at + step)), axis=0) for step in (0, 8)], axis=0
            )
            rows = pl.ds(pl.multiple_of(at, PAD), PAD)
            cols_ref[rows, :] = value.astype(BF16)
            square_ref[rows, :] = (value * value).astype(BF16)


def build_rows(row_start_ref, row_weights_ref, flip_ref, rows_ref, square_ref):
    flip_ref[...] = jnp.zeros_like(flip_ref)
    for tap in range(TAPS):
        flip_ref[tap : tap + 1, :] = row_weights_ref[tap]
    flip_ref[8:9, :] = row_start_ref[...].astype(F32)
    for block in range(ROWS // LANES):
        at = slice(block * LANES, (block + 1) * LANES)
        turned = jnp.transpose(flip_ref[:, at])
        lane = lax.broadcasted_iota(jnp.int32, (LANES, LANES), 1)
        base = lane - turned[:, 8:9].astype(jnp.int32)
        for part in range(ROWS // LANES):
            value = jnp.take_along_axis(turned, nth_tap(base + part * LANES), axis=1)
            lanes = slice(part * LANES, (part + 1) * LANES)
            rows_ref[at, lanes] = value.astype(BF16)
            square_ref[at, lanes] = (value * value).astype(BF16)


def half_start(side):
    core = lax.axis_index("visit") % 2
    half = (core + 1 - side) % 2
    return half, pl.multiple_of(half * (ROWS - REACH), PAD)


def edge_kernel(
    offset_ref, pixels_ref, noise_ref, col_start_ref, col_weights_ref, row_start_ref, row_weights_ref,
    send_ref, rest_ref, edge_ref, last_weight_ref, last_patch_ref, rows_ref, rows2_ref, low_ref, low2_ref, rolled_ref,
    table_ref, flip_ref, cols_ref, cols2_ref, held_ref, held2_ref, whole_ref,
    col_first_ref, col_taps_ref, row_first_ref, row_taps_ref, sems,
):
    loads = [
        pltpu.make_async_copy(source, target, sems.at[number])
        for number, (source, target) in enumerate(
            (
                (row_start_ref, row_first_ref),
                (row_weights_ref, row_taps_ref),
                (col_start_ref, col_first_ref),
                (col_weights_ref, col_taps_ref),
                (pixels_ref, held_ref),
                (noise_ref, held2_ref),
            )
        )
    ]
    for load in loads:
        load.start()
    shift = offset_ref[0, 0]
    for load in loads[:2]:
        load.wait()
    build_rows(row_first_ref, row_taps_ref, flip_ref, rows_ref, rows2_ref)
    for load in loads[2:4]:
        load.wait()
    table_ref[...] = jnp.zeros_like(table_ref)
    for tap in range(TAPS):
        table_ref[tap : tap + 1, :] = col_taps_ref[tap]
    table_ref[TAPS : TAPS + 1, :] = col_first_ref[...].astype(F32)
    table = pltpu.roll(table_ref[...], shift, 1)
    rolled_ref[...] = table
    parts = jnp.concatenate([table[:, :EDGE], table[:, COLS - LANES :]], axis=1)
    build_cols(parts, 0, EDGE + LANES, cols_ref, cols2_ref)
    loads[4].wait()
    low_ref[...] = held_ref[...].astype(BF16)
    across = dot(low_ref[...], cols_ref[...]).astype(BF16)
    loads[5].wait()
    low2_ref[...] = held2_ref[...].astype(BF16)
    across2 = dot(low2_ref[...], cols2_ref[...]).astype(BF16)
    warped = dot(rows_ref[...], across)
    inverse = 1.0 / dot(rows2_ref[...], across2)
    scaled = warped * inverse
    mine = lax.broadcasted_iota(jnp.int32, (ROWS, EDGE), 1) >= shift
    edge_scaled = scaled[:, :EDGE]
    edge_inverse = inverse[:, :EDGE]
    edge_ref[0:ROWS, :] = edge_scaled
    edge_ref[ROWS:, :] = edge_inverse
    whole_ref[0:ROWS, :] = jnp.where(mine, 0.0, edge_scaled).astype(BF16)
    whole_ref[ROWS:, :] = jnp.where(mine, 0.0, edge_inverse).astype(BF16)
    half, start = half_start(0)
    rest = pl.multiple_of((1 - half) * REACH, PAD)
    send_ref[0:REACH, :] = whole_ref[pl.ds(start, REACH), :]
    send_ref[REACH : 2 * REACH, :] = whole_ref[pl.ds(start + ROWS, REACH), :]
    rest_ref[0 : ROWS - REACH, :] = whole_ref[pl.ds(rest, ROWS - REACH), :]
    rest_ref[ROWS - REACH :, :] = whole_ref[pl.ds(rest + ROWS, ROWS - REACH), :]
    last_inverse = inverse[:, EDGE:]
    last = scaled[:, EDGE:] / jnp.maximum(last_inverse, 0.1)
    last_weight_ref[...] = last_inverse.astype(BF16)
    last_patch_ref[...] = last.astype(BF16)
    tail = jnp.transpose(last)[LANES - 16 :].astype(BF16)
    send_ref[2 * REACH : 2 * REACH + 16, :] = tail[:, :256]
    send_ref[2 * REACH + 16 :, :] = tail[:, 256:]


def middle_kernel(
    offset_ref, coef_ref, low_ref, low2_ref, rolled_ref, rows_ref, rows2_ref,
    last_patch_ref, last_weight_ref, factors_ref, edge_ref,
    patch_ref, weight_ref, taps_ref, head_ref, sent_ref,
    cols_ref, cols2_ref,
):
    turned = jnp.concatenate(
        [jnp.transpose(edge_ref[0:ROWS, :LANES])[0:16], jnp.transpose(edge_ref[ROWS:, :LANES])[0:16]], axis=0
    )
    column = lax.broadcasted_iota(jnp.int32, (32, ROWS), 0) % 16
    head_ref[...] = jnp.where(column >= offset_ref[0, 0], turned, 0.0).astype(BF16)
    sent_ref[...] = jnp.where(column >= offset_ref[0, 0], 0.0, turned)
    width = COLS - EDGE - LANES
    build_cols(rolled_ref[...], EDGE, width, cols_ref, cols2_ref)
    across = dot(low_ref[...], cols_ref[...]).astype(BF16)
    across2 = dot(low2_ref[...], cols2_ref[...]).astype(BF16)
    warped = dot(rows_ref[...], across)
    inverse = 1.0 / dot(rows2_ref[...], across2)
    patch = (warped * inverse) / jnp.maximum(inverse, 0.1)
    weight_ref[:, :width] = inverse.astype(BF16)
    weight_ref[:, width:] = last_weight_ref[...]
    wide = jnp.concatenate([patch, last_patch_ref[...].astype(F32), jnp.zeros((ROWS, LANES), F32)], axis=1)
    patch_ref[...] = pltpu.roll(wide, RADIUS, 1).astype(BF16)
    below = lax.broadcasted_iota(jnp.int32, (LANES, LANES), 1) <= lax.broadcasted_iota(jnp.int32, (LANES, LANES), 0)
    for b, terms in enumerate(kernel_terms()):
        line = sum(coef_ref[0, k] * factors_ref[a : a + 1, :] for k, a in terms)
        line = line.astype(BF16).astype(F32)
        spread = pltpu.roll(jnp.broadcast_to(line, (LANES, LANES)), 0, 1, stride=1, stride_axis=0)
        lanes = slice(b * LANES, (b + 1) * LANES)
        taps_ref[:LANES, lanes] = jnp.where(below, spread, 0.0).astype(BF16)
        taps_ref[LANES:, lanes] = jnp.where(below, 0.0, spread).astype(BF16)


def row_block(step):
    core = lax.axis_index("visit") % 2
    return pl.multiple_of(((step + 2 * core) % 4) * LANES, LANES)


def convolve(window, taps_ref, band_ref, along_ref):
    for half in range(2):
        source = window(half)
        for piece in range(FILTERS // 2):
            lanes = slice(piece * 2 * LANES, (piece + 1) * 2 * LANES)
            along = dot(source, taps_ref[:, lanes]).astype(BF16)
            at = slice(half * LANES, (half + 1) * LANES)
            along_ref[2 * piece, PAD : PAD + ROWS, at] = along[:, :LANES]
            along_ref[2 * piece + 1, PAD : PAD + ROWS, at] = along[:, LANES:]
    for step in range(ROWS // LANES):
        at = row_block(step)
        source = jnp.concatenate([along_ref[a, pl.ds(at, WINDOW), :] for a in range(FILTERS)], axis=0)
        yield step, at, dot(band_ref[...], source)


def clear_margins(along_ref):
    for a in range(FILTERS):
        along_ref[a, 0:PAD, :] = jnp.zeros((PAD, 2 * LANES), BF16)
        along_ref[a, PAD + ROWS :, :] = jnp.zeros((PAD, 2 * LANES), BF16)


def inner_kernel(patch_ref, weight_ref, taps_ref, band_ref, matched_ref, keep_ref, give_ref, along_ref):
    clear_margins(along_ref)
    halves = (keep_ref, keep_ref, give_ref, give_ref)
    for step in range(4):
        low = LANES * (step % 2)
        halves[step][low : low + LANES, 4 * LANES :] = weight_ref[pl.ds(row_block(step), LANES), :]

    @pl.loop(0, 2)
    def _(pair):
        start = pl.multiple_of(pair * 2 * LANES, 2 * LANES)

        def window(half):
            at = pl.multiple_of(start + LANES + half * LANES, LANES)
            return patch_ref[:, pl.ds(at, 2 * LANES)]

        for step, at, matched in convolve(window, taps_ref, band_ref, along_ref):
            rows = pl.ds(at, LANES)
            matched_ref[rows, pl.ds(start, 2 * LANES)] = matched
            weight = weight_ref[rows, pl.ds(pl.multiple_of(start + LANES, LANES), 2 * LANES)].astype(F32)
            low = LANES * (step % 2)
            halves[step][low : low + LANES, pl.ds(start, 2 * LANES)] = (weight * matched).astype(BF16)


def match_half(
    side, offset_ref, scaled, weights, edge_ref, patch_ref, weight_ref, left, right, taps_ref, band_ref,
    matched_ref, term_ref, along_ref, padded_ref, held_ref,
):
    half, start = half_start(side)
    window = pl.ds(start, REACH)
    inside = pl.multiple_of(half * PAD, PAD)
    for a in range(FILTERS):
        along_ref[a, 0:PAD, :] = jnp.zeros((PAD, 2 * LANES), BF16)
        along_ref[a, REACH:, :] = jnp.zeros((PAD, 2 * LANES), BF16)
    mine = lax.broadcasted_iota(jnp.int32, (REACH, EDGE), 1) >= offset_ref[0, 0]
    total_scaled = jnp.where(mine, edge_ref[window, :], 0.0) + scaled.astype(F32)
    total_weight = jnp.where(mine, edge_ref[pl.ds(start + ROWS, REACH), :], 0.0) + weights.astype(F32)
    patch = total_scaled / jnp.maximum(total_weight, 0.1)
    held_ref[:, :EDGE] = total_weight.astype(BF16)
    held_ref[:, EDGE:] = weight_ref[window, :]
    lane = lax.broadcasted_iota(jnp.int32, (REACH, LANES), 1)
    wide = pltpu.roll(jnp.concatenate([patch, left[window, :]], axis=1), RADIUS, 1)
    padded_ref[:, :EDGE] = wide[:, :EDGE].astype(BF16)
    padded_ref[:, EDGE : EDGE + LANES] = jnp.where(
        lane < RADIUS, wide[:, EDGE:], patch_ref[window, :LANES].astype(F32)
    ).astype(BF16)
    padded_ref[:, EDGE + LANES : COLS] = patch_ref[window, LANES : COLS - EDGE]
    padded_ref[:, COLS:] = jnp.where(
        (lane >= RADIUS) & (lane < 2 * RADIUS), right[window, :],
        jnp.where(lane < RADIUS, patch_ref[window, COLS - EDGE :].astype(F32), 0.0),
    ).astype(BF16)
    own = pl.ds(inside, ROWS // 2)
    term_ref[:, 4 * LANES :] = held_ref[own, :EDGE]

    @pl.loop(0, 2)
    def _(pair):
        def place(half):
            return pl.multiple_of(jnp.where(pair == 0, half, 2 + 5 * half) * LANES, LANES)

        for number in range(2):
            source = padded_ref[:, pl.ds(place(number), 2 * LANES)]
            at = slice(number * LANES, (number + 1) * LANES)
            rows = pl.ds(pl.multiple_of(PAD - inside, PAD), REACH)
            for piece in range(FILTERS // 2):
                along = dot(source, taps_ref[:, piece * 2 * LANES : (piece + 1) * 2 * LANES]).astype(BF16)
                along_ref[2 * piece, rows, at] = along[:, :LANES]
                along_ref[2 * piece + 1, rows, at] = along[:, LANES:]
        lanes = pl.ds(pl.multiple_of(pair * 2 * LANES, LANES), 2 * LANES)
        for step in range(2):
            at = slice(step * LANES, (step + 1) * LANES)
            source = jnp.concatenate(
                [along_ref[a, step * LANES : step * LANES + WINDOW, :] for a in range(FILTERS)], axis=0
            )
            matched = dot(band_ref[...], source)
            matched_ref[at, lanes] = matched
            rows = pl.ds(pl.multiple_of(inside + step * LANES, PAD), LANES)
            weight = jnp.concatenate([held_ref[rows, pl.ds(place(number), LANES)] for number in range(2)], axis=1)
            term_ref[at, lanes] = (weight.astype(F32) * matched).astype(BF16)


def given_kernel(
    offset_ref, got_ref, ahead_ref, edge_ref, sent_ref, patch_ref, weight_ref, taps_ref, band_ref,
    matched_ref, term_ref, left_ref, right_ref,
    along_ref, padded_ref, held_ref, flip_ref,
):
    flip_ref[...] = jnp.zeros_like(flip_ref)
    flip_ref[LANES - 16 :, :256] = got_ref[2 * REACH : 2 * REACH + 16, :].astype(F32)
    flip_ref[LANES - 16 :, 256:] = got_ref[2 * REACH + 16 :, :].astype(F32)
    left_ref[...] = jnp.transpose(flip_ref[...])
    near_scaled = ahead_ref[0:16, :].astype(F32) + sent_ref[0:16, :]
    near_weight = ahead_ref[16:32, :].astype(F32) + sent_ref[16:32, :]
    flip_ref[0:16, :] = near_scaled / jnp.maximum(near_weight, 0.1)
    right_ref[...] = pltpu.roll(jnp.transpose(flip_ref[...]), RADIUS, 1)
    match_half(
        0, offset_ref, got_ref[0:REACH, :], got_ref[REACH : 2 * REACH, :], edge_ref, patch_ref, weight_ref,
        left_ref, right_ref, taps_ref, band_ref, matched_ref, term_ref, along_ref, padded_ref, held_ref,
    )


def kept_kernel(
    offset_ref, got_ref, rest_ref, edge_ref, patch_ref, weight_ref, left_ref, right_ref, taps_ref, band_ref,
    matched_ref, term_ref,
    along_ref, padded_ref, held_ref, joined_ref,
):
    half, _ = half_start(1)
    count = ROWS - REACH
    both = REACH - count
    for part in range(2):
        there = pl.multiple_of(part * REACH + half * count, PAD)
        here = pl.multiple_of(part * REACH + (1 - half) * count, PAD)
        joined_ref[pl.ds(here, both), :] = got_ref[pl.ds(there, both), :]
        here = pl.multiple_of(part * REACH + half * both, PAD)
        joined_ref[pl.ds(here, count), :] = rest_ref[part * count : (part + 1) * count, :]
    match_half(
        1, offset_ref, joined_ref[0:REACH, :], joined_ref[REACH:, :], edge_ref, patch_ref, weight_ref,
        left_ref, right_ref, taps_ref, band_ref, matched_ref, term_ref, along_ref, padded_ref, held_ref,
    )


def pair_kernel(keep_ref, got_ref, keep2_ref, got2_ref, own_ref, two_ref, three_ref, one_ref):
    chip = lax.axis_index("visit") // 2
    width = keep_ref.shape[1]
    for ahead, out_ref in ((0, own_ref), (2, two_ref), (3, three_ref), (1, one_ref)):
        rows = pl.ds(pl.multiple_of(((chip + ahead) % 4) * PIECE, PIECE), PIECE)
        first = keep_ref[rows, :].astype(F32) + got_ref[rows, :].astype(F32)
        second = keep2_ref[rows, :].astype(F32) + got2_ref[rows, :].astype(F32)
        out_ref[:, :width] = first.astype(out_ref.dtype)
        out_ref[:, width:] = second.astype(out_ref.dtype)


def coadd_kernel(own_ref, one_ref, two_ref, three_ref, coadd_ref):
    total = own_ref[...] + one_ref[...].astype(F32) + two_ref[...].astype(F32) + three_ref[...].astype(F32)
    inner, outer = total[:, : COLS + 2 * LANES], total[:, COLS + 2 * LANES :]
    weight = jnp.maximum(jnp.concatenate([outer[:, 4 * LANES :], inner[:, 4 * LANES :]], axis=1), 0.1)
    terms = jnp.concatenate([outer[:, : 3 * LANES], inner[:, : 4 * LANES], outer[:, 3 * LANES : 4 * LANES]], axis=1)
    coadd_ref[...] = (terms / weight).astype(BF16)


def final_kernel(places, *refs):
    inner_ref, *outer_refs = refs[:3]
    difference_out, image_out, difference_ref, image_ref, sems = refs[-5:]
    index = lax.axis_index("visit")
    chip, core = index // 2, index % 2
    copies = []
    for number, (side, back) in enumerate(places):
        outer_ref = outer_refs[side]
        within = pl.multiple_of(((chip + 4 - back) % 4) * PIECE, PIECE)
        rows = pl.ds(pl.multiple_of(((core + side) % 2) * (4 * PIECE) + within, PIECE), PIECE)
        near = pl.ds(within, PIECE)
        image = refs[3 + number][...].astype(F32)
        image_ref[number] = image
        difference_ref[number, :, : 3 * LANES] = outer_ref[near, : 3 * LANES] - image[:, : 3 * LANES]
        difference_ref[number, :, 3 * LANES : 7 * LANES] = inner_ref[rows, :] - image[:, 3 * LANES : 7 * LANES]
        difference_ref[number, :, 7 * LANES :] = outer_ref[near, 3 * LANES :] - image[:, 7 * LANES :]
        for which, (held, out) in enumerate(((image_ref, image_out), (difference_ref, difference_out))):
            copy = pltpu.make_async_copy(held.at[number], out.at[rows, :], sems.at[which, number])
            copy.start()
            copies.append(copy)
    for copy in copies:
        copy.wait()


def finish(places, matched, pieces, done, name, moved):
    count = len(places)
    return call(
        functools.partial(final_kernel, places),
        [((ROWS, COLS), F32), ((ROWS, COLS), F32)],
        [pltpu.VMEM((count, PIECE, COLS), F32)] * 2 + [pltpu.SemaphoreType.DMA((2, count))],
        [VMEM_SPEC] * (3 + count) + [HBM_SPEC] * len(done),
        count * PIECE * COLS,
        moved,
        name,
        HBM_SPEC,
        {3 + count + i: i for i in range(len(done))},
    )(*matched, *pieces, *done)


def call(body, outs, scratch, specs, flops, moved, name, out_spec=None, aliases=None):
    return pl.pallas_call(
        body,
        out_shape=[jax.ShapeDtypeStruct(shape, dtype) for shape, dtype in outs],
        in_specs=specs,
        out_specs=[out_spec or VMEM_SPEC for _ in outs],
        scratch_shapes=scratch,
        input_output_aliases=aliases or {},
        compiler_params=pltpu.CompilerParams(vmem_limit_bytes=VMEM_LIMIT),
        cost_estimate=pl.CostEstimate(flops=flops, bytes_accessed=moved, transcendentals=0),
        name=name,
    )


SMEM_SPEC = pl.BlockSpec(memory_space=pltpu.SMEM)
VMEM_SPEC = pl.BlockSpec(memory_space=pltpu.VMEM)
HBM_SPEC = pl.BlockSpec(memory_space=pltpu.HBM)


def shifted(x, axis, by):
    size = lax.axis_size(axis)
    return lax.ppermute(x, axis, [(i, (i + by) % size) for i in range(size)])


def in_hbm(x):
    return pltpu.with_memory_space_constraint(x, pltpu.HBM)


def partner(x):
    return lax.ppermute(x, "visit", [(i, i ^ 1) for i in range(lax.axis_size("visit"))])


def per_device(
    exposure, variance, col_start, col_weights, row_start, row_weights, offsets, basis_coef
):
    pixels = in_hbm(exposure[0])
    noise = in_hbm(variance[0])
    col_taps = in_hbm(jnp.transpose(col_weights, (1, 0, 2)))
    row_taps = in_hbm(jnp.transpose(row_weights, (1, 0, 2)))
    col_start = in_hbm(col_start)
    row_start = in_hbm(row_start)
    factors = np.zeros((16, LANES), np.float32)
    factors[:FILTERS, : 2 * RADIUS + 1] = factor_table()
    factors = np.roll(factors, -2 * RADIUS, axis=1)
    band = jnp.asarray(row_band())
    width = EDGE + LANES
    send, rest, edge, last_weight, last_patch, rows, rows2, low, low2, rolled = call(
        edge_kernel,
        [
            ((2 * REACH + 32, EDGE), BF16),
            ((2 * (ROWS - REACH), EDGE), BF16),
            ((2 * ROWS, EDGE), F32),
            ((ROWS, LANES), BF16),
            ((ROWS, LANES), BF16),
            ((ROWS, ROWS), BF16),
            ((ROWS, ROWS), BF16),
            ((ROWS, COLS), BF16),
            ((ROWS, COLS), BF16),
            ((8, COLS), F32),
        ],
        [
            pltpu.VMEM((8, COLS), F32),
            pltpu.VMEM((LANES, ROWS), F32),
            pltpu.VMEM((COLS, width), BF16),
            pltpu.VMEM((COLS, width), BF16),
            pltpu.VMEM((ROWS, COLS), F32),
            pltpu.VMEM((ROWS, COLS), F32),
            pltpu.VMEM((2 * ROWS, EDGE), BF16),
            pltpu.VMEM((1, COLS), jnp.int32),
            pltpu.VMEM((TAPS, 1, COLS), F32),
            pltpu.VMEM((1, ROWS), jnp.int32),
            pltpu.VMEM((TAPS, 1, ROWS), F32),
            pltpu.SemaphoreType.DMA((6,)),
        ],
        [SMEM_SPEC] + [HBM_SPEC] * 6,
        4 * ROWS * width * (COLS + ROWS),
        8 << 20,
        "edge_columns",
    )(offsets, pixels, noise, col_start, col_taps, row_start, row_taps)
    got = shifted(send, "patch", 1)
    got_rest = shifted(rest, "patch", 1)
    width = COLS - EDGE - LANES
    patch, weight, taps, head, sent = call(
        middle_kernel,
        [
            ((ROWS, COLS - EDGE + LANES), BF16),
            ((ROWS, COLS - EDGE), BF16),
            ((2 * LANES, FILTERS * LANES), BF16),
            ((32, ROWS), BF16),
            ((32, ROWS), F32),
        ],
        [pltpu.VMEM((COLS, width), BF16), pltpu.VMEM((COLS, width), BF16)],
        [SMEM_SPEC] * 2 + [VMEM_SPEC] * 9,
        1 << 20,
        1 << 10,
        "middle_columns",
    )(offsets, basis_coef, low, low2, rolled, rows, rows2, last_patch, last_weight, jnp.asarray(factors), edge)
    ahead = shifted(head, "patch", -1)
    conv_flops = 2 * ROWS * ROWS * FILTERS * (2 * LANES + WINDOW)
    inner_width = COLS + 2 * LANES
    inner, keep, give = call(
        inner_kernel,
        [((ROWS, 4 * LANES), F32), ((ROWS // 2, inner_width), BF16), ((ROWS // 2, inner_width), BF16)],
        [pltpu.VMEM((FILTERS, ROWS + 2 * PAD, 2 * LANES), BF16)],
        [VMEM_SPEC] * 4,
        1 << 20,
        1 << 10,
        "inner_match",
    )(patch, weight, taps, band)
    inner_sum = keep, partner(give)
    outer_width = 4 * LANES + EDGE
    half_outs = [((ROWS // 2, 4 * LANES), F32), ((ROWS // 2, outer_width), BF16)]
    half_scratch = [
        pltpu.VMEM((FILTERS, REACH + PAD, 2 * LANES), BF16),
        pltpu.VMEM((REACH, COLS + LANES), BF16),
        pltpu.VMEM((REACH, COLS), BF16),
    ]
    given, give, left, right = call(
        given_kernel,
        half_outs + [((ROWS, LANES), F32)] * 2,
        half_scratch + [pltpu.VMEM((LANES, ROWS), F32)],
        [SMEM_SPEC] + [VMEM_SPEC] * 8,
        1 << 20,
        1 << 10,
        "given_match",
    )(offsets, got, ahead, edge, sent, patch, weight, taps, band)
    kept, keep = call(
        kept_kernel,
        half_outs,
        half_scratch + [pltpu.VMEM((2 * REACH, EDGE), BF16)],
        [SMEM_SPEC] + [VMEM_SPEC] * 9,
        8 * conv_flops,
        64 << 20,
        "kept_match",
    )(offsets, got, got_rest, edge, patch, weight, left, right, taps, band)
    own_piece, *others = call(
        pair_kernel,
        [((PIECE, inner_width + outer_width), F32)] + [((PIECE, inner_width + outer_width), BF16)] * 3,
        [],
        [VMEM_SPEC] * 4,
        ROWS * COLS,
        3 << 20,
        "pair_sum",
    )(*inner_sum, keep, partner(give))
    others = [shifted(x, "visit", 2 * ahead) for ahead, x in zip((2, 3, 1), others)]
    (piece,) = call(
        coadd_kernel, [((PIECE, COLS), BF16)], [], [VMEM_SPEC] * 4, 8 * PIECE * COLS, 2 << 20, "coadd"
    )(own_piece, *others)
    backs = (1, 3, 2)
    column = [shifted(piece, "visit", 2 * ahead) for ahead in backs]
    matched = inner, kept, given
    done = finish(((0, 0),), matched, [piece], [], "difference_near", 1 << 20)
    *done, column[2] = lax.optimization_barrier((*done, column[2]))
    swapped = [partner(x) for x in [piece, *column]]
    done = finish(tuple((0, back) for back in backs), matched, column, done, "difference_own", 64 << 20)
    difference, image = finish(tuple((1, back) for back in (0, *backs)), matched, swapped, done, "difference_other", 3 << 20)
    return (difference[None], image)


def solution(mesh):
    return jax.shard_map(
        per_device,
        mesh=mesh,
        in_specs=(
            P("visit", None, "patch"),
            P("visit", None, "patch"),
            P("visit", "patch"),
            P("visit", None, "patch"),
            P("visit", "patch"),
            P("visit", None, "patch"),
            P("visit", "patch"),
            P("visit", None),
        ),
        out_specs=(P("visit", None, "patch"), P(None, "patch")),
        check_vma=False,
    )
```

```python
import functools
import math

import jax
import jax.numpy as jnp
import numpy as np
from jax import lax
from jax.experimental import pallas as pl
from jax.experimental.pallas import tpu as pltpu
from jax.sharding import PartitionSpec as P

RADIUS = 10
TAPS = 6
ROWS = 512
COLS = 1024
EDGE = 256
LANES = 128
FILTERS = 12
WINDOW = 160
PAD = 16
REACH = 272
PIECE = 64
SPREADS = (0.7, 1.5, 3.0)
DEGREES = (4, 3, 2)
F32 = jnp.float32
BF16 = jnp.bfloat16
VMEM_LIMIT = 28 * 1024 * 1024


def factor_table():
    distance = np.arange(2 * RADIUS + 1).astype(np.float32) - RADIUS
    rows = []
    for spread, degree in zip(SPREADS, DEGREES):
        gaussian = np.exp(-distance * distance / np.float32(2.0 * spread * spread)) / np.float32(
            spread * math.sqrt(2.0 * math.pi)
        )
        for exponent in range(degree + 1):
            rows.append(gaussian * (distance / np.float32(spread)) ** exponent)
    return np.stack(rows).astype(np.float32)


def kernel_terms():
    terms = [[] for _ in range(FILTERS)]
    kernel = 0
    first = 0
    for degree in DEGREES:
        for i in range(degree + 1):
            for j in range(degree + 1 - i):
                terms[first + j].append((kernel, first + i))
                kernel += 1
        first += degree + 1
    return terms


def row_band():
    factors = factor_table().astype(BF16)
    gap = np.arange(LANES)[:, None] + PAD - np.arange(WINDOW)[None, :]
    inside = np.abs(gap) <= RADIUS
    at = np.clip(gap + RADIUS, 0, 2 * RADIUS)
    band = np.where(inside[None], factors[:, at], np.zeros((), BF16))
    return band.transpose(1, 0, 2).reshape(LANES, FILTERS * WINDOW).astype(BF16)


def dot(a, b):
    return jnp.dot(a, b, preferred_element_type=F32)


def nth_tap(gap):
    return jnp.where((gap & -8) == 0, gap, 7)


def build_cols(table, low, width, cols_ref, square_ref):
    taps = table[:, low : low + width]
    first = taps[TAPS : TAPS + 1].astype(jnp.int32)
    taps = jnp.where(lax.broadcasted_iota(jnp.int32, (8, width), 0) < TAPS, taps, 0.0)
    base = lax.broadcasted_iota(jnp.int32, (8, width), 0) - first

    @pl.loop(0, COLS // LANES)
    def _(block):
        for group in range(LANES // PAD):
            at = block * LANES + group * PAD
            value = jnp.concatenate(
                [jnp.take_along_axis(taps, nth_tap(base + (at + step)), axis=0) for step in (0, 8)], axis=0
            )
            rows = pl.ds(pl.multiple_of(at, PAD), PAD)
            cols_ref[rows, :] = value.astype(BF16)
            square_ref[rows, :] = (value * value).astype(BF16)


def build_rows(row_start_ref, row_weights_ref, flip_ref, rows_ref, square_ref):
    flip_ref[...] = jnp.zeros_like(flip_ref)
    for tap in range(TAPS):
        flip_ref[tap : tap + 1, :] = row_weights_ref[tap]
    flip_ref[8:9, :] = row_start_ref[...].astype(F32)
    for block in range(ROWS // LANES):
        at = slice(block * LANES, (block + 1) * LANES)
        turned = jnp.transpose(flip_ref[:, at])
        lane = lax.broadcasted_iota(jnp.int32, (LANES, LANES), 1)
        base = lane - turned[:, 8:9].astype(jnp.int32)
        for part in range(ROWS // LANES):
            value = jnp.take_along_axis(turned, nth_tap(base + part * LANES), axis=1)
            lanes = slice(part * LANES, (part + 1) * LANES)
            rows_ref[at, lanes] = value.astype(BF16)
            square_ref[at, lanes] = (value * value).astype(BF16)


def half_start(side):
    core = lax.axis_index("visit") % 2
    half = (core + 1 - side) % 2
    return half, pl.multiple_of(half * (ROWS - REACH), PAD)


def edge_kernel(
    offset_ref, pixels_ref, noise_ref, col_start_ref, col_weights_ref, row_start_ref, row_weights_ref,
    send_ref, rest_ref, edge_ref, last_weight_ref, last_patch_ref, rows_ref, rows2_ref, low_ref, low2_ref, rolled_ref,
    table_ref, flip_ref, cols_ref, cols2_ref, held_ref, held2_ref, whole_ref,
    col_first_ref, col_taps_ref, row_first_ref, row_taps_ref, sems,
):
    loads = [
        pltpu.make_async_copy(source, target, sems.at[number])
        for number, (source, target) in enumerate(
            (
                (row_start_ref, row_first_ref),
                (row_weights_ref, row_taps_ref),
                (col_start_ref, col_first_ref),
                (col_weights_ref, col_taps_ref),
                (pixels_ref, held_ref),
                (noise_ref, held2_ref),
            )
        )
    ]
    for load in loads:
        load.start()
    shift = offset_ref[0, 0]
    for load in loads[:4]:
        load.wait()
    table_ref[...] = jnp.zeros_like(table_ref)
    for tap in range(TAPS):
        table_ref[tap : tap + 1, :] = col_taps_ref[tap]
    table_ref[TAPS : TAPS + 1, :] = col_first_ref[...].astype(F32)
    table = pltpu.roll(table_ref[...], shift, 1)
    rolled_ref[...] = table
    parts = jnp.concatenate([table[:, :EDGE], table[:, COLS - LANES :]], axis=1)
    build_cols(parts, 0, EDGE + LANES, cols_ref, cols2_ref)
    loads[4].wait()
    loads[5].wait()
    low_ref[...] = held_ref[...].astype(BF16)
    across = dot(low_ref[...], cols_ref[...]).astype(BF16)
    build_rows(row_first_ref, row_taps_ref, flip_ref, rows_ref, rows2_ref)
    low2_ref[...] = held2_ref[...].astype(BF16)
    across2 = dot(low2_ref[...], cols2_ref[...]).astype(BF16)
    warped = dot(rows_ref[...], across)
    inverse = 1.0 / dot(rows2_ref[...], across2)
    scaled = warped * inverse
    mine = lax.broadcasted_iota(jnp.int32, (ROWS, EDGE), 1) >= shift
    edge_scaled = scaled[:, :EDGE]
    edge_inverse = inverse[:, :EDGE]
    edge_ref[0:ROWS, :] = edge_scaled
    edge_ref[ROWS:, :] = edge_inverse
    whole_ref[0:ROWS, :] = jnp.where(mine, 0.0, edge_scaled).astype(BF16)
    whole_ref[ROWS:, :] = jnp.where(mine, 0.0, edge_inverse).astype(BF16)
    half, start = half_start(0)
    rest = pl.multiple_of((1 - half) * REACH, PAD)
    send_ref[0:REACH, :] = whole_ref[pl.ds(start, REACH), :]
    send_ref[REACH : 2 * REACH, :] = whole_ref[pl.ds(start + ROWS, REACH), :]
    rest_ref[0 : ROWS - REACH, :] = whole_ref[pl.ds(rest, ROWS - REACH), :]
    rest_ref[ROWS - REACH :, :] = whole_ref[pl.ds(rest + ROWS, ROWS - REACH), :]
    last_inverse = inverse[:, EDGE:]
    last = scaled[:, EDGE:] / jnp.maximum(last_inverse, 0.1)
    last_weight_ref[...] = last_inverse.astype(BF16)
    last_patch_ref[...] = last.astype(BF16)
    tail = jnp.transpose(last)[LANES - 16 :].astype(BF16)
    send_ref[2 * REACH : 2 * REACH + 16, :] = tail[:, :256]
    send_ref[2 * REACH + 16 :, :] = tail[:, 256:]


def middle_kernel(
    offset_ref, coef_ref, low_ref, low2_ref, rolled_ref, rows_ref, rows2_ref,
    last_patch_ref, last_weight_ref, factors_ref, edge_ref,
    patch_ref, weight_ref, taps_ref, head_ref, sent_ref,
    cols_ref, cols2_ref,
):
    turned = jnp.concatenate(
        [jnp.transpose(edge_ref[0:ROWS, :LANES])[0:16], jnp.transpose(edge_ref[ROWS:, :LANES])[0:16]], axis=0
    )
    column = lax.broadcasted_iota(jnp.int32, (32, ROWS), 0) % 16
    head_ref[...] = jnp.where(column >= offset_ref[0, 0], turned, 0.0).astype(BF16)
    sent_ref[...] = jnp.where(column >= offset_ref[0, 0], 0.0, turned)
    width = COLS - EDGE - LANES
    build_cols(rolled_ref[...], EDGE, width, cols_ref, cols2_ref)
    across = dot(low_ref[...], cols_ref[...]).astype(BF16)
    across2 = dot(low2_ref[...], cols2_ref[...]).astype(BF16)
    warped = dot(rows_ref[...], across)
    inverse = 1.0 / dot(rows2_ref[...], across2)
    patch = (warped * inverse) / jnp.maximum(inverse, 0.1)
    weight_ref[:, :width] = inverse.astype(BF16)
    weight_ref[:, width:] = last_weight_ref[...]
    wide = jnp.concatenate([patch, last_patch_ref[...].astype(F32), jnp.zeros((ROWS, LANES), F32)], axis=1)
    patch_ref[...] = pltpu.roll(wide, RADIUS, 1).astype(BF16)
    below = lax.broadcasted_iota(jnp.int32, (LANES, LANES), 1) <= lax.broadcasted_iota(jnp.int32, (LANES, LANES), 0)
    for b, terms in enumerate(kernel_terms()):
        line = sum(coef_ref[0, k] * factors_ref[a : a + 1, :] for k, a in terms)
        line = line.astype(BF16).astype(F32)
        spread = pltpu.roll(jnp.broadcast_to(line, (LANES, LANES)), 0, 1, stride=1, stride_axis=0)
        lanes = slice(b * LANES, (b + 1) * LANES)
        taps_ref[:LANES, lanes] = jnp.where(below, spread, 0.0).astype(BF16)
        taps_ref[LANES:, lanes] = jnp.where(below, 0.0, spread).astype(BF16)


def row_block(step):
    core = lax.axis_index("visit") % 2
    return pl.multiple_of(((step + 2 * core) % 4) * LANES, LANES)


def convolve(window, taps_ref, band_ref, along_ref):
    for half in range(2):
        source = window(half)
        for piece in range(FILTERS // 2):
            lanes = slice(piece * 2 * LANES, (piece + 1) * 2 * LANES)
            along = dot(source, taps_ref[:, lanes]).astype(BF16)
            at = slice(half * LANES, (half + 1) * LANES)
            along_ref[2 * piece, PAD : PAD + ROWS, at] = along[:, :LANES]
            along_ref[2 * piece + 1, PAD : PAD + ROWS, at] = along[:, LANES:]
    for step in range(ROWS // LANES):
        at = row_block(step)
        source = jnp.concatenate([along_ref[a, pl.ds(at, WINDOW), :] for a in range(FILTERS)], axis=0)
        yield step, at, dot(band_ref[...], source)


def clear_margins(along_ref):
    for a in range(FILTERS):
        along_ref[a, 0:PAD, :] = jnp.zeros((PAD, 2 * LANES), BF16)
        along_ref[a, PAD + ROWS :, :] = jnp.zeros((PAD, 2 * LANES), BF16)


def inner_kernel(patch_ref, weight_ref, taps_ref, band_ref, matched_ref, keep_ref, give_ref, along_ref):
    clear_margins(along_ref)
    halves = (keep_ref, keep_ref, give_ref, give_ref)
    for step in range(4):
        low = LANES * (step % 2)
        halves[step][low : low + LANES, 4 * LANES :] = weight_ref[pl.ds(row_block(step), LANES), :]

    @pl.loop(0, 2)
    def _(pair):
        start = pl.multiple_of(pair * 2 * LANES, 2 * LANES)

        def window(half):
            at = pl.multiple_of(start + LANES + half * LANES, LANES)
            return patch_ref[:, pl.ds(at, 2 * LANES)]

        for step, at, matched in convolve(window, taps_ref, band_ref, along_ref):
            rows = pl.ds(at, LANES)
            matched_ref[rows, pl.ds(start, 2 * LANES)] = matched
            weight = weight_ref[rows, pl.ds(pl.multiple_of(start + LANES, LANES), 2 * LANES)].astype(F32)
            low = LANES * (step % 2)
            halves[step][low : low + LANES, pl.ds(start, 2 * LANES)] = (weight * matched).astype(BF16)


def match_half(
    side, offset_ref, scaled, weights, edge_ref, patch_ref, weight_ref, left, right, taps_ref, band_ref,
    matched_ref, term_ref, along_ref, padded_ref, held_ref,
):
    half, start = half_start(side)
    window = pl.ds(start, REACH)
    inside = pl.multiple_of(half * PAD, PAD)
    for a in range(FILTERS):
        along_ref[a, 0:PAD, :] = jnp.zeros((PAD, 2 * LANES), BF16)
        along_ref[a, REACH:, :] = jnp.zeros((PAD, 2 * LANES), BF16)
    mine = lax.broadcasted_iota(jnp.int32, (REACH, EDGE), 1) >= offset_ref[0, 0]
    total_scaled = jnp.where(mine, edge_ref[window, :], 0.0) + scaled.astype(F32)
    total_weight = jnp.where(mine, edge_ref[pl.ds(start + ROWS, REACH), :], 0.0) + weights.astype(F32)
    patch = total_scaled / jnp.maximum(total_weight, 0.1)
    held_ref[:, :EDGE] = total_weight.astype(BF16)
    held_ref[:, EDGE:] = weight_ref[window, :]
    lane = lax.broadcasted_iota(jnp.int32, (REACH, LANES), 1)
    wide = pltpu.roll(jnp.concatenate([patch, left[window, :]], axis=1), RADIUS, 1)
    padded_ref[:, :EDGE] = wide[:, :EDGE].astype(BF16)
    padded_ref[:, EDGE : EDGE + LANES] = jnp.where(
        lane < RADIUS, wide[:, EDGE:], patch_ref[window, :LANES].astype(F32)
    ).astype(BF16)
    padded_ref[:, EDGE + LANES : COLS] = patch_ref[window, LANES : COLS - EDGE]
    padded_ref[:, COLS:] = jnp.where(
        (lane >= RADIUS) & (lane < 2 * RADIUS), right[window, :],
        jnp.where(lane < RADIUS, patch_ref[window, COLS - EDGE :].astype(F32), 0.0),
    ).astype(BF16)
    own = pl.ds(inside, ROWS // 2)
    term_ref[:, 4 * LANES :] = held_ref[own, :EDGE]

    @pl.loop(0, 2)
    def _(pair):
        def place(half):
            return pl.multiple_of(jnp.where(pair == 0, half, 2 + 5 * half) * LANES, LANES)

        for number in range(2):
            source = padded_ref[:, pl.ds(place(number), 2 * LANES)]
            at = slice(number * LANES, (number + 1) * LANES)
            rows = pl.ds(pl.multiple_of(PAD - inside, PAD), REACH)
            for piece in range(FILTERS // 2):
                along = dot(source, taps_ref[:, piece * 2 * LANES : (piece + 1) * 2 * LANES]).astype(BF16)
                along_ref[2 * piece, rows, at] = along[:, :LANES]
                along_ref[2 * piece + 1, rows, at] = along[:, LANES:]
        lanes = pl.ds(pl.multiple_of(pair * 2 * LANES, LANES), 2 * LANES)
        for step in range(2):
            at = slice(step * LANES, (step + 1) * LANES)
            source = jnp.concatenate(
                [along_ref[a, step * LANES : step * LANES + WINDOW, :] for a in range(FILTERS)], axis=0
            )
            matched = dot(band_ref[...], source)
            matched_ref[at, lanes] = matched
            rows = pl.ds(pl.multiple_of(inside + step * LANES, PAD), LANES)
            weight = jnp.concatenate([held_ref[rows, pl.ds(place(number), LANES)] for number in range(2)], axis=1)
            term_ref[at, lanes] = (weight.astype(F32) * matched).astype(BF16)


def given_kernel(
    offset_ref, got_ref, ahead_ref, edge_ref, sent_ref, patch_ref, weight_ref, taps_ref, band_ref,
    matched_ref, term_ref, left_ref, right_ref,
    along_ref, padded_ref, held_ref, flip_ref,
):
    flip_ref[...] = jnp.zeros_like(flip_ref)
    flip_ref[LANES - 16 :, :256] = got_ref[2 * REACH : 2 * REACH + 16, :].astype(F32)
    flip_ref[LANES - 16 :, 256:] = got_ref[2 * REACH + 16 :, :].astype(F32)
    left_ref[...] = jnp.transpose(flip_ref[...])
    near_scaled = ahead_ref[0:16, :].astype(F32) + sent_ref[0:16, :]
    near_weight = ahead_ref[16:32, :].astype(F32) + sent_ref[16:32, :]
    flip_ref[0:16, :] = near_scaled / jnp.maximum(near_weight, 0.1)
    right_ref[...] = pltpu.roll(jnp.transpose(flip_ref[...]), RADIUS, 1)
    match_half(
        0, offset_ref, got_ref[0:REACH, :], got_ref[REACH : 2 * REACH, :], edge_ref, patch_ref, weight_ref,
        left_ref, right_ref, taps_ref, band_ref, matched_ref, term_ref, along_ref, padded_ref, held_ref,
    )


def kept_kernel(
    offset_ref, got_ref, rest_ref, edge_ref, patch_ref, weight_ref, left_ref, right_ref, taps_ref, band_ref,
    matched_ref, term_ref,
    along_ref, padded_ref, held_ref, joined_ref,
):
    half, _ = half_start(1)
    count = ROWS - REACH
    both = REACH - count
    for part in range(2):
        there = pl.multiple_of(part * REACH + half * count, PAD)
        here = pl.multiple_of(part * REACH + (1 - half) * count, PAD)
        joined_ref[pl.ds(here, both), :] = got_ref[pl.ds(there, both), :]
        here = pl.multiple_of(part * REACH + half * both, PAD)
        joined_ref[pl.ds(here, count), :] = rest_ref[part * count : (part + 1) * count, :]
    match_half(
        1, offset_ref, joined_ref[0:REACH, :], joined_ref[REACH:, :], edge_ref, patch_ref, weight_ref,
        left_ref, right_ref, taps_ref, band_ref, matched_ref, term_ref, along_ref, padded_ref, held_ref,
    )


def pair_kernel(keep_ref, got_ref, keep2_ref, got2_ref, own_ref, two_ref, one_ref, three_ref):
    chip = lax.axis_index("visit") // 2
    width = keep_ref.shape[1]
    for ahead, out_ref in ((0, own_ref), (2, two_ref), (1, one_ref), (3, three_ref)):
        rows = pl.ds(pl.multiple_of(((chip + ahead) % 4) * PIECE, PIECE), PIECE)
        first = keep_ref[rows, :].astype(F32) + got_ref[rows, :].astype(F32)
        second = keep2_ref[rows, :].astype(F32) + got2_ref[rows, :].astype(F32)
        out_ref[:, :width] = first.astype(out_ref.dtype)
        out_ref[:, width:] = second.astype(out_ref.dtype)


def coadd_kernel(own_ref, one_ref, two_ref, three_ref, coadd_ref):
    total = own_ref[...] + one_ref[...].astype(F32) + two_ref[...].astype(F32) + three_ref[...].astype(F32)
    inner, outer = total[:, : COLS + 2 * LANES], total[:, COLS + 2 * LANES :]
    weight = jnp.maximum(jnp.concatenate([outer[:, 4 * LANES :], inner[:, 4 * LANES :]], axis=1), 0.1)
    terms = jnp.concatenate([outer[:, : 3 * LANES], inner[:, : 4 * LANES], outer[:, 3 * LANES : 4 * LANES]], axis=1)
    coadd_ref[...] = (terms / weight).astype(BF16)


def final_kernel(places, *refs):
    inner_ref, *outer_refs = refs[:3]
    difference_out, image_out, difference_ref, image_ref, sems = refs[-5:]
    index = lax.axis_index("visit")
    chip, core = index // 2, index % 2
    copies = []
    for number, (side, back) in enumerate(places):
        outer_ref = outer_refs[side]
        within = pl.multiple_of(((chip + 4 - back) % 4) * PIECE, PIECE)
        rows = pl.ds(pl.multiple_of(((core + side) % 2) * (4 * PIECE) + within, PIECE), PIECE)
        near = pl.ds(within, PIECE)
        image = refs[3 + number][...].astype(F32)
        image_ref[number] = image
        difference_ref[number, :, : 3 * LANES] = outer_ref[near, : 3 * LANES] - image[:, : 3 * LANES]
        difference_ref[number, :, 3 * LANES : 7 * LANES] = inner_ref[rows, :] - image[:, 3 * LANES : 7 * LANES]
        difference_ref[number, :, 7 * LANES :] = outer_ref[near, 3 * LANES :] - image[:, 7 * LANES :]
        for which, (held, out) in enumerate(((image_ref, image_out), (difference_ref, difference_out))):
            copy = pltpu.make_async_copy(held.at[number], out.at[rows, :], sems.at[which, number])
            copy.start()
            copies.append(copy)
    for copy in copies:
        copy.wait()


def finish(places, matched, pieces, done, name, moved):
    count = len(places)
    return call(
        functools.partial(final_kernel, places),
        [((ROWS, COLS), F32), ((ROWS, COLS), F32)],
        [pltpu.VMEM((count, PIECE, COLS), F32)] * 2 + [pltpu.SemaphoreType.DMA((2, count))],
        [VMEM_SPEC] * (3 + count) + [HBM_SPEC] * len(done),
        count * PIECE * COLS,
        moved,
        name,
        HBM_SPEC,
        {3 + count + i: i for i in range(len(done))},
    )(*matched, *pieces, *done)


def call(body, outs, scratch, specs, flops, moved, name, out_spec=None, aliases=None):
    return pl.pallas_call(
        body,
        out_shape=[jax.ShapeDtypeStruct(shape, dtype) for shape, dtype in outs],
        in_specs=specs,
        out_specs=[out_spec or VMEM_SPEC for _ in outs],
        scratch_shapes=scratch,
        input_output_aliases=aliases or {},
        compiler_params=pltpu.CompilerParams(vmem_limit_bytes=VMEM_LIMIT),
        cost_estimate=pl.CostEstimate(flops=flops, bytes_accessed=moved, transcendentals=0),
        name=name,
    )


SMEM_SPEC = pl.BlockSpec(memory_space=pltpu.SMEM)
VMEM_SPEC = pl.BlockSpec(memory_space=pltpu.VMEM)
HBM_SPEC = pl.BlockSpec(memory_space=pltpu.HBM)


def shifted(x, axis, by):
    size = lax.axis_size(axis)
    return lax.ppermute(x, axis, [(i, (i + by) % size) for i in range(size)])


def in_hbm(x):
    return pltpu.with_memory_space_constraint(x, pltpu.HBM)


def partner(x):
    return lax.ppermute(x, "visit", [(i, i ^ 1) for i in range(lax.axis_size("visit"))])


def per_device(
    exposure, variance, col_start, col_weights, row_start, row_weights, offsets, basis_coef
):
    pixels = in_hbm(exposure[0])
    noise = in_hbm(variance[0])
    col_taps = in_hbm(jnp.transpose(col_weights, (1, 0, 2)))
    row_taps = in_hbm(jnp.transpose(row_weights, (1, 0, 2)))
    col_start = in_hbm(col_start)
    row_start = in_hbm(row_start)
    factors = np.zeros((16, LANES), np.float32)
    factors[:FILTERS, : 2 * RADIUS + 1] = factor_table()
    factors = np.roll(factors, -2 * RADIUS, axis=1)
    band = jnp.asarray(row_band())
    width = EDGE + LANES
    send, rest, edge, last_weight, last_patch, rows, rows2, low, low2, rolled = call(
        edge_kernel,
        [
            ((2 * REACH + 32, EDGE), BF16),
            ((2 * (ROWS - REACH), EDGE), BF16),
            ((2 * ROWS, EDGE), F32),
            ((ROWS, LANES), BF16),
            ((ROWS, LANES), BF16),
            ((ROWS, ROWS), BF16),
            ((ROWS, ROWS), BF16),
            ((ROWS, COLS), BF16),
            ((ROWS, COLS), BF16),
            ((8, COLS), F32),
        ],
        [
            pltpu.VMEM((8, COLS), F32),
            pltpu.VMEM((LANES, ROWS), F32),
            pltpu.VMEM((COLS, width), BF16),
            pltpu.VMEM((COLS, width), BF16),
            pltpu.VMEM((ROWS, COLS), F32),
            pltpu.VMEM((ROWS, COLS), F32),
            pltpu.VMEM((2 * ROWS, EDGE), BF16),
            pltpu.VMEM((1, COLS), jnp.int32),
            pltpu.VMEM((TAPS, 1, COLS), F32),
            pltpu.VMEM((1, ROWS), jnp.int32),
            pltpu.VMEM((TAPS, 1, ROWS), F32),
            pltpu.SemaphoreType.DMA((6,)),
        ],
        [SMEM_SPEC] + [HBM_SPEC] * 6,
        4 * ROWS * width * (COLS + ROWS),
        8 << 20,
        "edge_columns",
    )(offsets, pixels, noise, col_start, col_taps, row_start, row_taps)
    got = shifted(send, "patch", 1)
    got_rest = shifted(rest, "patch", 1)
    width = COLS - EDGE - LANES
    patch, weight, taps, head, sent = call(
        middle_kernel,
        [
            ((ROWS, COLS - EDGE + LANES), BF16),
            ((ROWS, COLS - EDGE), BF16),
            ((2 * LANES, FILTERS * LANES), BF16),
            ((32, ROWS), BF16),
            ((32, ROWS), F32),
        ],
        [pltpu.VMEM((COLS, width), BF16), pltpu.VMEM((COLS, width), BF16)],
        [SMEM_SPEC] * 2 + [VMEM_SPEC] * 9,
        1 << 20,
        1 << 10,
        "middle_columns",
    )(offsets, basis_coef, low, low2, rolled, rows, rows2, last_patch, last_weight, jnp.asarray(factors), edge)
    ahead = shifted(head, "patch", -1)
    conv_flops = 2 * ROWS * ROWS * FILTERS * (2 * LANES + WINDOW)
    inner_width = COLS + 2 * LANES
    inner, keep, give = call(
        inner_kernel,
        [((ROWS, 4 * LANES), F32), ((ROWS // 2, inner_width), BF16), ((ROWS // 2, inner_width), BF16)],
        [pltpu.VMEM((FILTERS, ROWS + 2 * PAD, 2 * LANES), BF16)],
        [VMEM_SPEC] * 4,
        1 << 20,
        1 << 10,
        "inner_match",
    )(patch, weight, taps, band)
    inner_sum = keep, partner(give)
    outer_width = 4 * LANES + EDGE
    half_outs = [((ROWS // 2, 4 * LANES), F32), ((ROWS // 2, outer_width), BF16)]
    half_scratch = [
        pltpu.VMEM((FILTERS, REACH + PAD, 2 * LANES), BF16),
        pltpu.VMEM((REACH, COLS + LANES), BF16),
        pltpu.VMEM((REACH, COLS), BF16),
    ]
    given, give, left, right = call(
        given_kernel,
        half_outs + [((ROWS, LANES), F32)] * 2,
        half_scratch + [pltpu.VMEM((LANES, ROWS), F32)],
        [SMEM_SPEC] + [VMEM_SPEC] * 8,
        1 << 20,
        1 << 10,
        "given_match",
    )(offsets, got, ahead, edge, sent, patch, weight, taps, band)
    kept, keep = call(
        kept_kernel,
        half_outs,
        half_scratch + [pltpu.VMEM((2 * REACH, EDGE), BF16)],
        [SMEM_SPEC] + [VMEM_SPEC] * 9,
        8 * conv_flops,
        64 << 20,
        "kept_match",
    )(offsets, got, got_rest, edge, patch, weight, left, right, taps, band)
    own_piece, *others = call(
        pair_kernel,
        [((PIECE, inner_width + outer_width), F32)] + [((PIECE, inner_width + outer_width), BF16)] * 3,
        [],
        [VMEM_SPEC] * 4,
        ROWS * COLS,
        3 << 20,
        "pair_sum",
    )(*inner_sum, keep, partner(give))
    others = [shifted(x, "visit", 2 * ahead) for ahead, x in zip((2, 1, 3), others)]
    (piece,) = call(
        coadd_kernel, [((PIECE, COLS), BF16)], [], [VMEM_SPEC] * 4, 8 * PIECE * COLS, 2 << 20, "coadd"
    )(own_piece, *others)
    backs = (1, 3, 2)
    column = [shifted(piece, "visit", 2 * ahead) for ahead in backs]
    matched = inner, kept, given
    done = finish(((0, 0),), matched, [piece], [], "difference_near", 1 << 20)
    *done, column[2] = lax.optimization_barrier((*done, column[2]))
    swapped = [partner(x) for x in [piece, *column]]
    done = finish(tuple((0, back) for back in backs), matched, column, done, "difference_own", 64 << 20)
    difference, image = finish(tuple((1, back) for back in (0, *backs)), matched, swapped, done, "difference_other", 3 << 20)
    return (difference[None], image)


def solution(mesh):
    return jax.shard_map(
        per_device,
        mesh=mesh,
        in_specs=(
            P("visit", None, "patch"),
            P("visit", None, "patch"),
            P("visit", "patch"),
            P("visit", None, "patch"),
            P("visit", "patch"),
            P("visit", None, "patch"),
            P("visit", "patch"),
            P("visit", None),
        ),
        out_specs=(P("visit", None, "patch"), P(None, "patch")),
        check_vma=False,
    )
```
